32 devices in a mesh: groups: 2 (over y), rows: 4 (over z), cols: 2 (over core), futures: 2 (over x).
Axes of the slice: x: 2, y: 2, z: 4, core: 2. Of those that a mesh axis runs over, the one named last changes fastest.
Arguments:
- features: bfloat16 [256, 64, 256], P('futures', ('groups', 'rows'), 'cols'), parts along dimension 1, may hold values from -6 to 6
- trunk_weights: bfloat16 [2, 9, 256, 256], P(None, None, 'futures'), may hold values from -0.125 to 0.125
- head_weights: bfloat16 [8, 3, 256], replicated, may hold values from -0.375 to 0.375
- flow_target: float32 [2, 64, 256], P(None, ('groups', 'rows'), 'cols'), parts along dimension 1, may hold values from -6 to 6
- labels: int32 [64, 256], P(('groups', 'rows'), 'cols'), parts along dimension 0, may hold values 0 or 1
- winner: int32 [8, 32], P(('groups', 'rows'), 'cols'), parts along dimension 0, may hold values from 0 to 7
Outputs:
- loss: float32 [2], P('groups'), parts along dimension 0
- trunk_grad: float32 [4, 9, 256, 256], P('groups', None, 'futures'), parts along dimension 0
- head_grad: float32 [8, 6, 256], P('futures', 'groups'), parts along dimension 1
The draws below stay inside these ranges and needn't reach their ends.
There are 2 independent parts, one for each index of `groups`. The reference program is written for one: setup_inputs(seed, part) draws one part's arguments, and reference() takes and returns one part's arrays. A program takes and returns all parts, laid end to end along the dimension named above; an argument that names none is the same for every part. Nothing has to cross between parts.
Inputs may be any that keep to these rules, and one draw needn't show every extreme that they name: `winner`: the winning future of each block of 8 x 8 cells.
All inputs are finite; a program needn't handle non-finite values. No bound on the sum of `labels` on one device may be relied on, other than what follows from the above.
Results may differ from the reference program's by a relative error of at most 0.0045.
Values may be sent and summed in bfloat16 or wider, within the bound.
No kernel may reach another device: no remote copies, remote signals or barrier semaphores. Data moves between devices by JAX's collectives and lax.ppermute only.
A program may use at most 64 MiB of HBM per device.

```python
import math
import jax
import jax.numpy as jnp
from jax import lax

C = 256
FUT = 8
LAYERS = 2
BLK = 8
NH = 32
NW = 256


def plant(result, key, smallest, largest):
    index_at = [jax.random.randint(jax.random.fold_in(key, axis), (), 0, length) for axis, length in enumerate(result.shape)]
    widest = result.shape.index(max(result.shape))
    next_to = index_at[:widest] + [(index_at[widest] + 1) % result.shape[widest]] + index_at[widest + 1:]
    return result.at[tuple(index_at)].set(smallest).at[tuple(next_to)].set(largest)


def block_levels(stream_key, extent, shards, least, top_value):
    gain = 1.0
    for position, blocks in shards:
        draws = jax.random.uniform(jax.random.fold_in(jax.random.fold_in(stream_key, 6), position), (blocks,), jnp.float32, least / len(shards), top_value / len(shards))
        gain = gain * jnp.repeat(jnp.exp(draws), extent[position] // blocks).reshape((-1,) + (1,) * (len(extent) - 1 - position))
    return gain


def normal_values(stream_key, shape, scale, bound, cuts=(), kind=jnp.bfloat16):
    result = scale * jax.random.normal(stream_key, shape, jnp.float32)
    if cuts:
        result = result * block_levels(stream_key, shape, cuts, -0.22, 0.18)
    return jnp.clip(result, -bound, bound).astype(kind)


def setup_inputs(seed: int = 0, part: int = 0) -> dict:
    key_list = jax.random.split(jax.random.key(seed), 7)
    own_keys = jax.random.split(jax.random.fold_in(key_list[6], part), 7)
    features = normal_values(own_keys[0], (C, NH, NW), 1.0, 6.0, ((0, 2), (1, 4), (2, 2)))
    trunk_weights = normal_values(key_list[1], (LAYERS, 9, C, C), (9 * C) ** -0.5, 0.125, ((2, 2),))
    head_weights = normal_values(key_list[2], (FUT, 3, C), C ** -0.5, 0.375)
    flow_target = normal_values(own_keys[3], (2, NH, NW), 1.0, 6.0, ((1, 4), (2, 2)), jnp.float32)
    labels = plant((jax.random.randint(own_keys[4], (NH, NW), 0, 2) < 1).astype(jnp.int32), jax.random.fold_in(own_keys[4], 1), 0, 1)
    winner = plant(jax.random.randint(own_keys[5], (NH // BLK, NW // BLK), 0, FUT), jax.random.fold_in(own_keys[5], 1), 0, FUT - 1).astype(jnp.int32)
    return dict(features=features, trunk_weights=trunk_weights, head_weights=head_weights, flow_target=flow_target, labels=labels, winner=winner)


def conv_forward(padded, taps, height, width):
    total = jnp.zeros((taps.shape[1], height * width), jnp.float32)
    for offset in range(9):
        row_off = offset // 3
        col_off = offset % 3
        window = padded[:, row_off:row_off + height, col_off:col_off + width].reshape(padded.shape[0], height * width)
        total = total + jnp.dot(taps[offset], window, preferred_element_type=jnp.float32)
    return total.reshape(taps.shape[1], height, width)

def conv_backward(padded_grad, taps, height, width):
    total = jnp.zeros((taps.shape[2], height * width), jnp.float32)
    for offset in range(9):
        row_off = 2 - offset // 3
        col_off = 2 - offset % 3
        window = padded_grad[:, row_off:row_off + height, col_off:col_off + width].reshape(padded_grad.shape[0], height * width)
        total = total + lax.dot_general(taps[offset], window, (((0,), (0,)), ((), ())), preferred_element_type=jnp.float32)
    return total.reshape(taps.shape[2], height, width)

def weight_grad(grad, padded, height, width):
    flat = grad.reshape(grad.shape[0], height * width)
    pieces = []
    for offset in range(9):
        row_off = offset // 3
        col_off = offset % 3
        window = padded[:, row_off:row_off + height, col_off:col_off + width].reshape(padded.shape[0], height * width)
        pieces.append(lax.dot_general(flat, window, (((1,), (1,)), ((), ())), preferred_element_type=jnp.float32))
    return jnp.stack(pieces)

def silu_slope(pre):
    sigma = jax.nn.sigmoid(pre)
    return sigma * (1.0 + pre * (1.0 - sigma))

def losses_and_grads(heads, labels, flow_target, mask, scale):
    logit = heads[:, 0]
    target = labels.astype(jnp.float32)[None]
    first = heads[:, 1] - flow_target[0][None]
    second = heads[:, 2] - flow_target[1][None]
    cell = jax.nn.softplus(logit) - target * logit + 0.5 * (first * first + second * second)
    total = jnp.sum(mask * cell)
    d_logit = mask * (jax.nn.sigmoid(logit) - target) * scale
    d_first = mask * first * scale
    d_second = mask * second * scale
    grads = jnp.stack([d_logit, d_first, d_second], axis=1).astype(jnp.bfloat16)
    return (total, grads)

def reference(features, trunk_weights, head_weights, flow_target, labels, winner):
    height = features.shape[1]
    width = features.shape[2]
    cell_count = height * width
    scale = 1.0 / math.sqrt(cell_count)
    active = features
    saved_pads = []
    saved_pre = []
    for layer in range(LAYERS):
        padded = jnp.pad(active, ((0, 0), (1, 1), (1, 1)))
        pre = conv_forward(padded, trunk_weights[layer], height, width)
        active = jax.nn.silu(pre).astype(jnp.bfloat16)
        saved_pads.append(padded)
        saved_pre.append(pre)
    futures_n = head_weights.shape[0]
    flat_active = active.reshape(active.shape[0], height * width)
    heads = jnp.dot(head_weights.reshape(futures_n * 3, -1), flat_active, preferred_element_type=jnp.float32).reshape(futures_n, 3, height, width)
    block_ids = jnp.repeat(jnp.repeat(winner, BLK, axis=0), BLK, axis=1)
    mask = (block_ids[None] == jnp.arange(futures_n, dtype=jnp.int32)[:, None, None]).astype(jnp.float32)
    total, head_grads = losses_and_grads(heads, labels, flow_target, mask, scale)
    loss = (total / cell_count).reshape(1)
    flat_grads = head_grads.reshape(futures_n * 3, height * width)
    head_grad = lax.dot_general(flat_grads, flat_active, (((1,), (1,)), ((), ())), preferred_element_type=jnp.float32).reshape(futures_n, 3, -1)
    upstream = lax.dot_general(head_weights.reshape(futures_n * 3, -1), flat_grads, (((0,), (0,)), ((), ())), preferred_element_type=jnp.float32).reshape(-1, height, width)
    trunk_parts = [None] * LAYERS
    for layer in reversed(range(LAYERS)):
        slope_grad = (upstream * silu_slope(saved_pre[layer])).astype(jnp.bfloat16)
        trunk_parts[layer] = weight_grad(slope_grad, saved_pads[layer], height, width)
        if layer > 0:
            padded_grad = jnp.pad(slope_grad, ((0, 0), (1, 1), (1, 1)))
            upstream = conv_backward(padded_grad, trunk_weights[layer], height, width)
    return (loss, jnp.stack(trunk_parts), head_grad)
```

```python
import functools
import math

import jax
import jax.numpy as jnp
from jax import lax
from jax.experimental import pallas as pl
from jax.experimental.pallas import tpu as pltpu
from jax.sharding import PartitionSpec as P

BLK = 8
SLOT = 16
F32 = jnp.float32
BF16 = jnp.bfloat16
VMEM = pl.BlockSpec(memory_space=pltpu.VMEM)
SMEM = pl.BlockSpec(memory_space=pltpu.SMEM)
PARAMS = pltpu.CompilerParams(vmem_limit_bytes=48 * 1024 * 1024)


def swap(block, axis, distance=1):
    count = lax.axis_size(axis)
    return lax.ppermute(block, axis, [(i, i ^ distance) for i in range(count)])


def shift(block, axis, step):
    count = lax.axis_size(axis)
    pairs = [(i, i + step) for i in range(count) if 0 <= i + step < count]
    return lax.ppermute(block, axis, pairs)


def ordered(flag, first, second, axis):
    return jnp.concatenate(
        [jnp.where(flag, second, first), jnp.where(flag, first, second)], axis=axis
    )


def pieces(total, step):
    return [(lo, min(step, total - lo)) for lo in range(0, total, step)]


def forward_taps(taps_ref, mat_ref):
    channels = taps_ref.shape[1]
    for tap in range(9):
        row, col = tap // 3, tap % 3
        mat_ref[
            row * channels : (row + 1) * channels, col * channels : (col + 1) * channels
        ] = taps_ref[tap].T


def clear_ends(low_ref, high_ref, count):
    blank = jnp.zeros((8, low_ref.shape[1]), F32)
    low_ref[:8, :] = blank
    high_ref[8 + count : 16 + count, :] = blank


def convolve(src_ref, mat_ref, low_ref, mid_ref, high_ref, count, stride):
    channels = src_ref.shape[1]
    clear_ends(low_ref, high_ref, count)
    for lo, size in pieces(count, 448):
        rows = jnp.concatenate(
            [src_ref[lo + row * stride : lo + row * stride + size, :] for row in range(3)], axis=1
        )
        for col, ref in enumerate((low_ref, mid_ref, high_ref)):
            ref[8 + lo : 8 + lo + size, :] = jnp.dot(
                rows,
                mat_ref[:, col * channels : (col + 1) * channels],
                preferred_element_type=F32,
            )


def combined(low_ref, mid_ref, high_ref, lo, size):
    return (
        low_ref[7 + lo : 7 + lo + size, :]
        + mid_ref[8 + lo : 8 + lo + size, :]
        + high_ref[9 + lo : 9 + lo + size, :]
    )


def own_part(value, index, count):
    width = value.shape[1] // count
    result = value[:, :width]
    for part in range(1, count):
        result = jnp.where(index == part, value[:, part * width : (part + 1) * width], result)
    return result


def kernel_grads(grad_ref, src_ref, base, stride, out_ref):
    own = grad_ref.shape[1]
    cells = grad_ref.shape[0]
    turned = grad_ref[...].T
    moved = jnp.concatenate(
        [
            pltpu.roll(turned, cells - 1, 1).astype(BF16),
            turned.astype(BF16),
            pltpu.roll(turned, 1, 1).astype(BF16),
        ],
        axis=0,
    )
    for row in range(3):
        start = base + row * stride
        part = jnp.dot(moved, src_ref[start : start + cells, :], preferred_element_type=F32)
        for col in range(3):
            tap = 3 * row + col
            out_ref[tap * own : (tap + 1) * own, :] = part[col * own : (col + 1) * own, :]


def first_layer(geom, scal, mid, top, bottom, tiles, taps, padded, active, slope, mat, low, cen, high):
    height, width, futs, layers = geom
    stride = width + SLOT
    halo = layers + 1
    col = scal[1]
    row_at = scal[2]
    row_count = scal[3]
    slots = height + 2 * halo
    lane = lax.broadcasted_iota(jnp.int32, tiles.shape[1:], 0)
    near = (lane < SLOT // 2).astype(jnp.int32) != col
    blank = jnp.zeros(tiles.shape[1:], BF16)
    padded[:SLOT, :] = jnp.where(near & (col == 1), tiles[0], blank)
    for row in range(slots):
        at = SLOT + row * stride
        if row < halo:
            source = top[row]
        elif row < halo + height:
            source = mid[row - halo]
        else:
            source = bottom[row - halo - height]
        padded[at : at + width, :] = source
        after = tiles[row + 1] if row + 1 < slots else blank
        padded[at + width : at + stride, :] = jnp.where(
            near, jnp.where(col == 1, after, tiles[row]), blank
        )
    forward_taps(taps, mat)
    count = active.shape[0]
    convolve(padded, mat, low, cen, high, count, stride)
    spot = lax.broadcasted_iota(jnp.int32, (stride, active.shape[1]), 0)
    inside = (spot < width) | ((col == 0) & (spot < width + SLOT // 2)) | (
        (col == 1) & (spot >= width + SLOT // 2)
    )

    bump = ((spot >= width) & (col == 1)).astype(jnp.int32)

    def finish(at, size, keep):
        pre = combined(low, cen, high, at, size)
        sigma = jax.nn.sigmoid(pre)
        active[at : at + size, :] = jnp.where(keep, pre * sigma, 0.0).astype(BF16)
        return pre, sigma

    edge = halo - 1
    finish(0, SLOT, (col == 1) & (row_at * height - edge >= 0))
    for row in range(height + 2 * edge):
        at = SLOT + row * stride
        place = row_at * height + row - edge
        keep = inside & (bump + place >= 0) & (bump + place < row_count * height)
        pre, sigma = finish(at, stride, keep)
        if edge <= row < edge + height:
            mine = (row - edge) * width
            own_pre = own_part(pre[:width], scal[0], futs)
            own_sig = own_part(sigma[:width], scal[0], futs)
            slope[mine : mine + width, :] = own_sig * (1.0 + own_pre * (1.0 - own_sig))


def last_layer(
    geom, scale, scal, active, taps, heads_w, aux, grad, taps_grad, head_grad, loss,
    mat, low, cen, high, out, pre_s, own_grad
):
    height, width, futs, layers = geom
    stride = width + SLOT
    count = grad.shape[0]
    forward_taps(taps, mat)
    convolve(active, mat, low, cen, high, count, stride)
    for lo, size in pieces(count, 208):
        pre = combined(low, cen, high, lo, size)
        pre_s[lo : lo + size, :] = pre
        out[lo : lo + size, :] = (pre * jax.nn.sigmoid(pre)).astype(BF16)
    nfut = heads_w.shape[0] // 3
    heads = lax.dot_general(
        heads_w[...], out[...], (((1,), (1,)), ((), ())), preferred_element_type=F32
    )
    logit = heads[:nfut]
    target = aux[0:1, :]
    first = heads[nfut : 2 * nfut] - aux[1:2, :]
    second = heads[2 * nfut :] - aux[2:3, :]
    future = lax.broadcasted_iota(jnp.int32, logit.shape, 0).astype(F32)
    mask = jnp.where(aux[3:4, :] == future, aux[4:5, :], 0.0)
    cell = (
        jnp.maximum(logit, 0.0)
        + jnp.log1p(jnp.exp(-jnp.abs(logit)))
        - target * logit
        + 0.5 * (first * first + second * second)
    )
    own = aux[5:6, :]
    loss[...] = jnp.broadcast_to(
        jnp.sum(jnp.where(mask * own > 0.0, cell, 0.0)), loss.shape
    )
    picked = mask > 0.0
    grads = jnp.concatenate(
        [
            jnp.where(picked, (jax.nn.sigmoid(logit) - target) * scale, 0.0),
            jnp.where(picked, first * scale, 0.0),
            jnp.where(picked, second * scale, 0.0),
        ],
        axis=0,
    )
    mine = jnp.where(own > 0.0, grads, 0.0).astype(BF16)
    grads = grads.astype(BF16)
    head_grad[...] = jnp.dot(mine, out[...], preferred_element_type=F32)
    up = lax.dot_general(
        grads, heads_w[...], (((0,), (0,)), ((), ())), preferred_element_type=F32
    )
    low[: count, :] = up
    own_grad[...] = jnp.zeros_like(own_grad)

    def back(lo, size):
        pre = pre_s[lo : lo + size, :]
        sigma = jax.nn.sigmoid(pre)
        value = (low[lo : lo + size, :] * (sigma * (1.0 + pre * (1.0 - sigma)))).astype(BF16)
        grad[lo : lo + size, :] = value
        return value

    back(0, SLOT)
    for row in range(height + 2):
        at = SLOT + row * stride
        value = back(at, stride)
        if 1 <= row <= height:
            mine_at = SLOT + (row - 1) * stride
            own_grad[mine_at : mine_at + width, :] = own_part(
                value[:width].astype(F32), scal[0], futs
            )
    kernel_grads(own_grad, active, stride, stride, taps_grad)


def back_layer(
    geom, scal, grad, taps, slope, padded, taps_grad, mat, low, cen, high, own_grad
):
    height, width, futs, layers = geom
    stride = width + SLOT
    channels = taps.shape[2]
    own = channels // futs
    count = SLOT + height * stride
    for tap in range(9):
        row, col = tap // 3, tap % 3
        mat[
            (2 - row) * channels : (3 - row) * channels, (2 - col) * own : (3 - col) * own
        ] = own_part(taps[tap], scal[0], futs)
    clear_ends(low, high, count)
    for lo, size in pieces(count, 400):
        rows = jnp.concatenate(
            [grad[lo + row * stride : lo + row * stride + size, :] for row in range(3)], axis=1
        )
        part = jnp.dot(rows, mat[...], preferred_element_type=F32)
        for col, ref in enumerate((low, cen, high)):
            ref[8 + lo : 8 + lo + size, :] = part[:, col * own : (col + 1) * own]
    own_grad[...] = jnp.zeros_like(own_grad)
    for row in range(height):
        at = SLOT + row * stride
        up = combined(low, cen, high, at, width)
        value = (up * slope[row * width : (row + 1) * width, :]).astype(BF16)
        own_grad[at : at + width, :] = value.astype(F32)
    kernel_grads(own_grad, padded, layers * stride, stride, taps_grad)


def other_taps(taps, core):
    half = taps.shape[1] // 2
    send = jnp.where(core == 0, taps[:, :half], taps[:, half:])
    got = swap(send, "futures")
    mate = swap(got, "cols")
    return ordered(core == 1, got, mate, 1)


def whole_taps(taps, fut, core):
    if lax.axis_size("futures") != 2:
        return lax.all_gather(taps, "futures", axis=1, tiled=True)
    return ordered(fut == 1, taps, other_taps(taps, core), 1)


def whole_channels(block, fut):
    if lax.axis_size("futures") != 2:
        return lax.all_gather(block, "futures", axis=block.ndim - 1, tiled=True)
    return ordered(fut == 1, block, swap(block, "futures"), block.ndim - 1)


def halves(block, flag):
    half = block.shape[0] // 2
    low, high = block[:half], block[half:]
    return jnp.where(flag, high, low), jnp.where(flag, low, high)


def tile_sum(block, core, row_at):
    kept, sent = halves(block, core == 1)
    kept = kept + swap(sent, "cols")
    bit = row_at & 1
    pair, sent = halves(kept, bit == 1)
    pair = pair + swap(rounded(sent).astype(BF16), "rows").astype(F32)
    pair = rounded(pair)
    done = (pair + swap(pair.astype(BF16), "rows", 2).astype(F32)).astype(BF16)
    done = ordered(bit == 1, done, swap(done, "rows"), 0)
    return ordered(core == 1, done, swap(done, "cols"), 0).astype(F32)


def small_sum(block):
    block = block + swap(block, "cols")
    block = block + swap(block, "rows")
    return block + swap(block, "rows", 2)


def rounded(value):
    return lax.reduce_precision(value, 8, 7)


def split3(value):
    high = rounded(value)
    rest = value - high
    mid = rounded(rest)
    return [high.astype(BF16), mid.astype(BF16), rounded(rest - mid).astype(BF16)]


def cell_data(labels, flow_target, winner, core, row_at, rows_total):
    height, width = labels.shape
    blocks = jnp.repeat(jnp.repeat(winner, BLK, axis=0), BLK, axis=1)
    planes = jnp.stack(
        [labels.astype(BF16), blocks.astype(BF16)]
        + split3(flow_target[0])
        + split3(flow_target[1])
    )
    above = shift(planes[:, -1], "rows", 1)[:, None]
    below = shift(planes[:, 0], "rows", -1)[:, None]
    planes = jnp.concatenate([above, planes, below], axis=1)
    edge = jnp.where(core == 0, planes[:, :, -SLOT:], planes[:, :, :SLOT])
    tile = swap(edge, "cols")
    count = height + 2
    blank = jnp.zeros_like(tile[:, :1])
    slots = jnp.where(
        core == 0,
        jnp.concatenate([blank, tile], axis=1),
        jnp.concatenate([tile, blank], axis=1),
    )
    rows = jnp.concatenate([planes, jnp.zeros_like(planes[:, :1])], axis=1)
    flat = jnp.concatenate([slots, rows], axis=2).astype(F32)
    flat = flat.reshape(flat.shape[0], -1)
    stride = width + SLOT
    total = SLOT + count * stride
    flat = flat[:, :total]
    line = jnp.arange(count + 1, dtype=jnp.int32)[:, None] - 1
    spot = jnp.arange(stride, dtype=jnp.int32)[None] - SLOT
    main = spot >= 0
    right = (core == 0) & (spot == -SLOT)
    left = (core == 1) & (spot == -1)
    line = jnp.where(right, line - 1, line)
    at = row_at * height + line
    real = (at >= 0) & (at < rows_total * height) & (line >= -1) & (line <= height)
    valid = (real & (main | right | left)).astype(F32).reshape(-1)[:total]
    own = (main & (line >= 0) & (line < height)).astype(F32).reshape(-1)[:total]
    return jnp.stack(
        [
            flat[0],
            flat[2] + flat[3] + flat[4],
            flat[5] + flat[6] + flat[7],
            flat[1],
            valid,
            own,
            jnp.zeros_like(own),
            jnp.zeros_like(own),
        ]
    )


def local(features, trunk_weights, head_weights, flow_target, labels, winner):
    own, height, width = features.shape
    layers, _, _, channels = trunk_weights.shape
    fut_total = head_weights.shape[0]
    futs = lax.axis_size("futures")
    fut_here = fut_total // futs
    rows_total = lax.axis_size("rows")
    fut = lax.axis_index("futures")
    core = lax.axis_index("cols")
    row_at = lax.axis_index("rows")
    cell_count = height * width * rows_total * lax.axis_size("cols")
    scale = 1.0 / math.sqrt(cell_count)
    halo = layers + 1
    stride = width + SLOT
    geom = (height, width, futs, layers)
    scal = jnp.stack([fut, core, row_at, jnp.int32(rows_total)]).astype(jnp.int32)

    mine = jnp.transpose(features, (1, 2, 0))
    mid = whole_channels(mine, fut)
    taps = [whole_taps(trunk_weights[layer], fut, core) for layer in range(layers)]
    top = shift(mid[-halo:], "rows", 1)
    bottom = shift(mid[:halo], "rows", -1)
    edge_of = lambda block: jnp.where(core == 0, block[:, -SLOT:], block[:, :SLOT])
    tiles = swap(
        jnp.concatenate([edge_of(top), edge_of(mid), edge_of(bottom)], axis=0), "cols"
    )
    aux = cell_data(labels, flow_target, winner, core, row_at, rows_total)
    heads_w = jnp.transpose(head_weights, (1, 0, 2)).reshape(3 * fut_total, channels)

    def cells(rows):
        return SLOT + rows * stride

    first_cells = cells(height + 4)
    last_cells = cells(height + 2)
    own_cells = -(-cells(height) // 128) * 128
    shape = jax.ShapeDtypeStruct
    padded, active, slope = pl.pallas_call(
        functools.partial(first_layer, geom),
        out_shape=(
            shape((cells(height + 6), channels), BF16),
            shape((first_cells, channels), BF16),
            shape((height * width, own), F32),
        ),
        in_specs=[SMEM] + [VMEM] * 5,
        out_specs=(VMEM,) * 3,
        scratch_shapes=[pltpu.VMEM((3 * channels, 3 * channels), BF16)]
        + [pltpu.VMEM((first_cells + 16, channels), F32)] * 3,
        compiler_params=PARAMS,
        name="first_layer",
    )(scal, mid, top, bottom, tiles, taps[0])

    grad, last_grads, head_grads, loss = pl.pallas_call(
        functools.partial(last_layer, geom, scale),
        out_shape=(
            shape((last_cells, channels), BF16),
            shape((9 * own, channels), F32),
            shape((3 * fut_total, channels), F32),
            shape((8, channels), F32),
        ),
        in_specs=[SMEM] + [VMEM] * 4,
        out_specs=(VMEM,) * 4,
        scratch_shapes=[pltpu.VMEM((3 * channels, 3 * channels), BF16)]
        + [pltpu.VMEM((last_cells + 16, channels), F32)] * 3
        + [
            pltpu.VMEM((last_cells, channels), BF16),
            pltpu.VMEM((last_cells, channels), F32),
            pltpu.VMEM((own_cells, own), F32),
        ],
        compiler_params=PARAMS,
        name="last_layer",
    )(scal, active, taps[1], heads_w, aux)

    first_grads = pl.pallas_call(
        functools.partial(back_layer, geom),
        out_shape=shape((9 * own, channels), F32),
        in_specs=[SMEM] + [VMEM] * 4,
        out_specs=VMEM,
        scratch_shapes=[pltpu.VMEM((3 * channels, 3 * own), BF16)]
        + [pltpu.VMEM((cells(height) + 16, own), F32)] * 3
        + [pltpu.VMEM((own_cells, own), F32)],
        compiler_params=PARAMS,
        name="back_layer",
    )(scal, grad, taps[1], slope, padded)

    by_fut = head_grads.reshape(3, fut_total, channels)
    by_fut = lax.dynamic_slice_in_dim(by_fut, fut * fut_here, fut_here, 1)
    small = jnp.concatenate([by_fut.reshape(3 * fut_here, channels), loss[:1]], axis=0)
    if rows_total == 4:
        sums = [tile_sum(block, core, row_at) for block in (last_grads, first_grads)][::-1]
        small = small_sum(small)
    else:
        sums = [lax.psum(block, ("rows", "cols")) for block in (first_grads, last_grads)]
        small = lax.psum(small, ("rows", "cols"))
    trunk_grad = jnp.stack(sums).reshape(layers, 9, own, channels)
    head_grad = jnp.transpose(small[:-1].reshape(3, fut_here, channels), (1, 0, 2))
    total = small[-1, :1] / cell_count
    return (total, trunk_grad, head_grad)


def solution(mesh):
    placed = (
        P("futures", ("groups", "rows"), "cols"),
        P(None, None, "futures", None),
        P(),
        P(None, ("groups", "rows"), "cols"),
        P(("groups", "rows"), "cols"),
        P(("groups", "rows"), "cols"),
    )
    return jax.shard_map(
        local,
        mesh=mesh,
        in_specs=placed,
        out_specs=(P("groups"), P("groups", None, "futures", None), P("futures", "groups", None)),
        check_vma=False,
    )
```

```python
import functools
import math

import jax
import jax.numpy as jnp
from jax import lax
from jax.experimental import pallas as pl
from jax.experimental.pallas import tpu as pltpu
from jax.sharding import PartitionSpec as P

BLK = 8
SLOT = 16
F32 = jnp.float32
BF16 = jnp.bfloat16
VMEM = pl.BlockSpec(memory_space=pltpu.VMEM)
SMEM = pl.BlockSpec(memory_space=pltpu.SMEM)
PARAMS = pltpu.CompilerParams(vmem_limit_bytes=14 * 1024 * 1024)


def swap(block, axis, distance=1):
    count = lax.axis_size(axis)
    return lax.ppermute(block, axis, [(i, i ^ distance) for i in range(count)])


def shift(block, axis, step):
    count = lax.axis_size(axis)
    pairs = [(i, i + step) for i in range(count) if 0 <= i + step < count]
    return lax.ppermute(block, axis, pairs)


def ordered(flag, first, second, axis):
    return jnp.concatenate(
        [jnp.where(flag, second, first), jnp.where(flag, first, second)], axis=axis
    )


def pieces(total, step):
    return [(lo, min(step, total - lo)) for lo in range(0, total, step)]


def whole_tap(layer, tap, scal, refs):
    if len(refs) == 1:
        return refs[0][tap]
    own_ref, got_ref, mate_ref = refs
    mine, got, mate = own_ref[layer, tap], got_ref[tap], mate_ref[tap]
    theirs = ordered(scal[1] == 1, got, mate, 0)
    return ordered(scal[0] == 1, mine, theirs, 0)


def forward_taps(layer, scal, refs, mat_ref):
    for tap in range(9):
        row, col = tap // 3, tap % 3
        block = whole_tap(layer, tap, scal, refs).T
        channels = block.shape[0]
        mat_ref[
            row * channels : (row + 1) * channels, col * channels : (col + 1) * channels
        ] = block


def clear_ends(low_ref, high_ref, count):
    blank = jnp.zeros((8, low_ref.shape[1]), F32)
    low_ref[:8, :] = blank
    high_ref[8 + count : 16 + count, :] = blank


def convolve(src_ref, mat_ref, low_ref, mid_ref, high_ref, count, stride):
    channels = src_ref.shape[1]
    clear_ends(low_ref, high_ref, count)
    for lo, size in pieces(count, 448):
        rows = jnp.concatenate(
            [src_ref[lo + row * stride : lo + row * stride + size, :] for row in range(3)], axis=1
        )
        for col, ref in enumerate((low_ref, mid_ref, high_ref)):
            ref[8 + lo : 8 + lo + size, :] = jnp.dot(
                rows,
                mat_ref[:, col * channels : (col + 1) * channels],
                preferred_element_type=F32,
            )


def combined(low_ref, mid_ref, high_ref, lo, size):
    return (
        low_ref[7 + lo : 7 + lo + size, :]
        + mid_ref[8 + lo : 8 + lo + size, :]
        + high_ref[9 + lo : 9 + lo + size, :]
    )


def own_part(value, index, count):
    width = value.shape[1] // count
    result = value[:, :width]
    for part in range(1, count):
        result = jnp.where(index == part, value[:, part * width : (part + 1) * width], result)
    return result


def kernel_grads(core, grad_ref, src_ref, base, stride, kept_ref, sent_ref):
    own = grad_ref.shape[1]
    cells = grad_ref.shape[0]
    turned = grad_ref[...].T
    moved = jnp.concatenate(
        [
            pltpu.roll(turned, cells - 1, 1).astype(BF16),
            turned.astype(BF16),
            pltpu.roll(turned, 1, 1).astype(BF16),
        ],
        axis=0,
    )
    for row in range(3):
        start = base + row * stride
        part = jnp.dot(moved, src_ref[start : start + cells, :], preferred_element_type=F32)
        for col in range(3):
            tap = 3 * row + col
            half = own // 2
            low = part[col * own : col * own + half, :]
            high = part[col * own + half : (col + 1) * own, :]
            kept_ref[tap] = jnp.where(core == 1, high, low)
            sent_ref[tap] = jnp.where(core == 1, low, high)


def prepare(scal, labels, flow, winner, taps, lines, *refs):
    layers = taps.shape[0]
    sends, sems = refs[:-1], refs[-1]
    copies = []
    for layer, send in enumerate(sends):
        half = send.shape[1]
        part = taps.at[layer, :, pl.ds(pl.multiple_of(scal[1] * half, half), half), :]
        copies.append(pltpu.make_async_copy(part, send, sems.at[layer]))
        copies[-1].start()
    height, width = labels.shape
    blocks = winner.shape[1]
    at = lax.broadcasted_iota(jnp.int32, (blocks, width), 1)
    block = lax.broadcasted_iota(jnp.int32, (blocks, width), 0)
    spread = ((at >= block * BLK) & (at < block * BLK + BLK)).astype(BF16)
    fields = [labels[...].astype(F32)]
    ids = [
        jnp.dot(winner[row : row + 1, :].astype(F32).astype(BF16), spread, preferred_element_type=F32)
        for row in range(height // BLK)
    ]
    fields.append(jnp.concatenate([jnp.broadcast_to(part, (BLK, width)) for part in ids], axis=0))
    for index in range(2):
        rest = flow[index]
        for _ in range(3):
            piece = rest.astype(BF16).astype(F32)
            fields.append(piece)
            rest = rest - piece
    for row in range(height):
        lines[row] = jnp.concatenate([field[row : row + 1] for field in fields], axis=0).astype(BF16)
    for copy in copies:
        copy.wait()


def first_layer(geom, scal, mid, top, bottom, tiles, *refs):
    taps = refs[:-7]
    padded, active, slope, mat, low, cen, high = refs[-7:]
    height, width, futs, layers = geom
    stride = width + SLOT
    halo = layers + 1
    col = scal[1]
    row_at = scal[2]
    row_count = scal[3]
    slots = height + 2 * halo
    lane = lax.broadcasted_iota(jnp.int32, tiles.shape[1:], 0)
    near = (lane < SLOT // 2).astype(jnp.int32) != col
    blank = jnp.zeros(tiles.shape[1:], BF16)
    padded[:SLOT, :] = jnp.where(near & (col == 1), tiles[0], blank)
    for row in range(slots):
        at = SLOT + row * stride
        if row < halo:
            source = top[row]
        elif row < halo + height:
            source = mid[row - halo]
        else:
            source = bottom[row - halo - height]
        padded[at : at + width, :] = source
        after = tiles[row + 1] if row + 1 < slots else blank
        padded[at + width : at + stride, :] = jnp.where(
            near, jnp.where(col == 1, after, tiles[row]), blank
        )
    forward_taps(0, scal, taps, mat)
    count = active.shape[0]
    convolve(padded, mat, low, cen, high, count, stride)
    spot = lax.broadcasted_iota(jnp.int32, (stride, active.shape[1]), 0)
    inside = (spot < width) | ((col == 0) & (spot < width + SLOT // 2)) | (
        (col == 1) & (spot >= width + SLOT // 2)
    )

    bump = ((spot >= width) & (col == 1)).astype(jnp.int32)

    def finish(at, size, keep):
        pre = combined(low, cen, high, at, size)
        sigma = jax.nn.sigmoid(pre)
        active[at : at + size, :] = jnp.where(keep, pre * sigma, 0.0).astype(BF16)
        return pre, sigma

    edge = halo - 1
    finish(0, SLOT, (col == 1) & (row_at * height - edge >= 0))
    for row in range(height + 2 * edge):
        at = SLOT + row * stride
        place = row_at * height + row - edge
        keep = inside & (bump + place >= 0) & (bump + place < row_count * height)
        pre, sigma = finish(at, stride, keep)
        if edge <= row < edge + height:
            mine = (row - edge) * width
            own_pre = own_part(pre[:width], scal[0], futs)
            own_sig = own_part(sigma[:width], scal[0], futs)
            slope[mine : mine + width, :] = own_sig * (1.0 + own_pre * (1.0 - own_sig))


def cell_data(scal, lines, above, below, tile, height, width):
    stride = width + SLOT
    count = height + 2
    core, row_at, row_count = scal[1], scal[2], scal[3]
    rows = [above[...]] + [lines[row] for row in range(height)] + [below[...]]
    blank = jnp.zeros(tile.shape[1:], F32)
    tiles = [blank] + [tile[row].astype(F32) for row in range(count)] + [blank]
    parts = []
    for row in range(count + 1):
        parts.append(jnp.where(core == 1, tiles[row + 1], tiles[row]))
        if row < count:
            parts.append(rows[row].astype(F32))
    flat = jnp.concatenate(parts, axis=1)
    place = lax.broadcasted_iota(jnp.int32, (8, flat.shape[1]), 1)
    line = jnp.full_like(place, -2)
    spot = place
    for row in range(count + 1):
        begin = row * stride
        line = jnp.where(place >= begin, row - 1, line)
        spot = jnp.where(place >= begin, place - (begin + SLOT), spot)
    main = spot >= 0
    right = (spot == -SLOT) & (core == 0)
    left = (spot == -1) & (core == 1)
    own = main & (line >= 0) & (line < height)
    line = line - right.astype(jnp.int32)
    at = row_at * height + line
    real = (at >= 0) & (at < row_count * height) & (line >= -1) & (line <= height)
    valid = real & (main | right | left)
    return (
        flat[0:1],
        flat[2:3] + flat[3:4] + flat[4:5],
        flat[5:6] + flat[6:7] + flat[7:8],
        flat[1:2],
        jnp.where(valid, 1.0, 0.0)[:1],
        jnp.where(own, 1.0, 0.0)[:1],
    )


def last_layer(
    geom, scale, scal, active, slope, padded, heads_w, lines, above, below, tile, *refs
):
    taps = refs[:-14]
    kept, sent, first_kept, first_sent, small = refs[-14:-9]
    mat, low, cen, high, out, pre_s, grad, own_grad, back_mat = refs[-9:]
    height, width, futs, layers = geom
    stride = width + SLOT
    count = grad.shape[0]
    forward_taps(layers - 1, scal, taps, mat)
    convolve(active, mat, low, cen, high, count, stride)
    for lo, size in pieces(count, 208):
        pre = combined(low, cen, high, lo, size)
        pre_s[lo : lo + size, :] = pre
        out[lo : lo + size, :] = (pre * jax.nn.sigmoid(pre)).astype(BF16)
    nfut = heads_w.shape[0] // 3
    heads = lax.dot_general(
        heads_w[...], out[...], (((1,), (1,)), ((), ())), preferred_element_type=F32
    )
    logit = heads[:nfut]
    target, flow_one, flow_two, picks, valid, own = cell_data(
        scal, lines, above, below, tile, height, width
    )
    first = heads[nfut : 2 * nfut] - flow_one
    second = heads[2 * nfut :] - flow_two
    future = lax.broadcasted_iota(jnp.int32, logit.shape, 0).astype(F32)
    mask = jnp.where(picks == future, valid, 0.0)
    cell = (
        jnp.maximum(logit, 0.0)
        + jnp.log1p(jnp.exp(-jnp.abs(logit)))
        - target * logit
        + 0.5 * (first * first + second * second)
    )
    loss = jnp.sum(jnp.where(mask * own > 0.0, cell, 0.0))
    picked = mask > 0.0
    grads = jnp.concatenate(
        [
            jnp.where(picked, (jax.nn.sigmoid(logit) - target) * scale, 0.0),
            jnp.where(picked, first * scale, 0.0),
            jnp.where(picked, second * scale, 0.0),
        ],
        axis=0,
    )
    mine = jnp.where(own > 0.0, grads, 0.0).astype(BF16)
    grads = grads.astype(BF16)
    by_head = jnp.dot(mine, out[...], preferred_element_type=F32)
    fut_here = nfut // futs
    lines = []
    for index in range(fut_here):
        for kind in range(3):
            at = kind * nfut + index
            line = by_head[at : at + 1, :]
            for part in range(1, futs):
                other = at + part * fut_here
                line = jnp.where(scal[0] == part, by_head[other : other + 1, :], line)
            lines.append(line)
    lines.append(jnp.broadcast_to(loss, (small.shape[0] - len(lines), small.shape[1])))
    small[...] = jnp.concatenate(lines, axis=0)
    up = lax.dot_general(
        grads, heads_w[...], (((0,), (0,)), ((), ())), preferred_element_type=F32
    )
    low[: count, :] = up
    own_grad[...] = jnp.zeros_like(own_grad)

    def back(lo, size):
        pre = pre_s[lo : lo + size, :]
        sigma = jax.nn.sigmoid(pre)
        value = (low[lo : lo + size, :] * (sigma * (1.0 + pre * (1.0 - sigma)))).astype(BF16)
        grad[lo : lo + size, :] = value
        return value

    back(0, SLOT)
    for row in range(height + 2):
        at = SLOT + row * stride
        value = back(at, stride)
        if 1 <= row <= height:
            mine_at = SLOT + (row - 1) * stride
            own_grad[mine_at : mine_at + width, :] = own_part(
                value[:width].astype(F32), scal[0], futs
            )
    kernel_grads(scal[1], own_grad, active, stride, stride, kept, sent)
    back_layer(
        geom, scal, grad, taps, slope, padded, first_kept, first_sent, back_mat, low, cen, high,
        own_grad,
    )


def back_layer(
    geom, scal, grad, taps, slope, padded, kept, sent, mat, low, cen, high, own_grad
):
    height, width, futs, layers = geom
    stride = width + SLOT
    channels = grad.shape[1]
    own = channels // futs
    count = SLOT + height * stride
    for tap in range(9):
        row, col = tap // 3, tap % 3
        mat[
            (2 - row) * channels : (3 - row) * channels, (2 - col) * own : (3 - col) * own
        ] = own_part(whole_tap(layers - 1, tap, scal, taps), scal[0], futs)
    low[:8, :own] = jnp.zeros((8, own), F32)
    high[8 + count : 16 + count, :own] = jnp.zeros((8, own), F32)
    for lo, size in pieces(count, 400):
        rows = jnp.concatenate(
            [grad[lo + row * stride : lo + row * stride + size, :] for row in range(3)], axis=1
        )
        part = jnp.dot(rows, mat[...], preferred_element_type=F32)
        for col, ref in enumerate((low, cen, high)):
            ref[8 + lo : 8 + lo + size, :own] = part[:, col * own : (col + 1) * own]
    own_grad[...] = jnp.zeros_like(own_grad)
    for row in range(height):
        at = SLOT + row * stride
        up = (
            low[7 + at : 7 + at + width, :own]
            + cen[8 + at : 8 + at + width, :own]
            + high[9 + at : 9 + at + width, :own]
        )
        value = (up * slope[row * width : (row + 1) * width, :]).astype(BF16)
        own_grad[at : at + width, :] = value.astype(F32)
    kernel_grads(scal[1], own_grad, padded, layers * stride, stride, kept, sent)


def tap_parts(taps, layer, send):
    if lax.axis_size("futures") != 2:
        return (lax.all_gather(taps[layer], "futures", axis=1, tiled=True),)
    got = swap(send, "futures")
    return (taps, got, swap(got, "cols"))


def tied(*blocks):
    return lax.optimization_barrier(blocks)


def tile_sums(last, first, small, core, row_at):
    bit = row_at & 1

    def over_cols(block, extra):
        kept, sent = block
        if extra is None:
            return kept + swap(sent, "cols"), None
        sent, extra = tied(sent, extra)
        got, more = tied(swap(sent, "cols"), swap(extra, "cols"))
        return kept + got, extra + more

    def over_pairs(block, extra):
        half = block.shape[1] // 2
        low, high = block[:, :half], block[:, half:]
        kept, sent = jnp.where(bit == 1, high, low), jnp.where(bit == 1, low, high)
        sent = rounded(sent).astype(BF16)
        if extra is None:
            return rounded(kept + swap(sent, "rows").astype(F32)), None
        sent, extra = tied(sent, extra)
        got, more = tied(swap(sent, "rows"), swap(extra, "rows"))
        return rounded(kept + got.astype(F32)), extra + more

    def over_ends(block, extra):
        sent = block.astype(BF16)
        if extra is None:
            return (block + swap(sent, "rows", 2).astype(F32)).astype(BF16), None
        sent, extra = tied(sent, extra)
        got, more = tied(swap(sent, "rows", 2), swap(extra, "rows", 2))
        return (block + got.astype(F32)).astype(BF16), extra + more

    for step in (over_cols, over_pairs, over_ends):
        last, small = step(last, small)
        first, _ = step(first, None)
    last, first = [ordered(bit == 1, block, swap(block, "rows"), 1) for block in (last, first)]
    last, first = [ordered(core == 1, block, swap(block, "cols"), 1) for block in (last, first)]
    return last.astype(F32), first.astype(F32), small


def rounded(value):
    return lax.reduce_precision(value, 8, 7)


def local(features, trunk_weights, head_weights, flow_target, labels, winner):
    own, height, width = features.shape
    layers, _, _, channels = trunk_weights.shape
    fut_total = head_weights.shape[0]
    futs = lax.axis_size("futures")
    fut_here = fut_total // futs
    rows_total = lax.axis_size("rows")
    fut = lax.axis_index("futures")
    core = lax.axis_index("cols")
    row_at = lax.axis_index("rows")
    cell_count = height * width * rows_total * lax.axis_size("cols")
    scale = 1.0 / math.sqrt(cell_count)
    halo = layers + 1
    stride = width + SLOT
    geom = (height, width, futs, layers)
    scal = jnp.stack([fut, core, row_at, jnp.int32(rows_total)]).astype(jnp.int32)

    shape = jax.ShapeDtypeStruct
    mine = jnp.transpose(features, (1, 2, 0))
    if futs == 2:
        theirs = swap(mine, "futures")
        mid = ordered(fut == 1, mine, theirs, 2)
    else:
        mid = lax.all_gather(mine, "futures", axis=2, tiled=True)
    lines, *sends = pl.pallas_call(
        prepare,
        out_shape=(shape((height, 8, width), BF16),)
        + (shape((9, own // 2, channels), BF16),) * layers,
        in_specs=[SMEM] + [VMEM] * 3 + [pl.BlockSpec(memory_space=pl.ANY)],
        out_specs=(VMEM,) * (1 + layers),
        scratch_shapes=[pltpu.SemaphoreType.DMA((layers,))],
        compiler_params=PARAMS,
        name="prepare",
    )(scal, labels, flow_target, winner, trunk_weights)
    taps = [tap_parts(trunk_weights, layer, sends[layer]) for layer in range(layers)]

    def with_line(block, line):
        line = jnp.pad(line, ((0, 0), (0, channels - width)))
        return jnp.concatenate([block.reshape(-1, channels), line], axis=0)

    top = shift(with_line(mid[-halo:], lines[-1]), "rows", 1)
    bottom = shift(with_line(mid[:halo], lines[0]), "rows", -1)
    rows = halo * width
    above, below = top[rows:, :width], bottom[rows:, :width]
    top = top[:rows].reshape(halo, width, channels)
    bottom = bottom[:rows].reshape(halo, width, channels)

    def edge_of(block):
        return jnp.where(core == 0, block[..., -SLOT:, :], block[..., :SLOT, :])

    tiles = swap(
        jnp.concatenate([edge_of(top), edge_of(mid), edge_of(bottom)], axis=0), "cols"
    )
    line_rows = jnp.concatenate([above[None], lines, below[None]], axis=0)
    tile = swap(
        jnp.where(core == 0, line_rows[:, :, -SLOT:], line_rows[:, :, :SLOT]), "cols"
    )
    heads_w = jnp.transpose(head_weights, (1, 0, 2)).reshape(3 * fut_total, channels)

    def cells(rows):
        return SLOT + rows * stride

    first_cells = cells(height + 4)
    last_cells = cells(height + 2)
    own_cells = -(-cells(height) // 128) * 128
    padded, active, slope = pl.pallas_call(
        functools.partial(first_layer, geom),
        out_shape=(
            shape((cells(height + 6), channels), BF16),
            shape((first_cells, channels), BF16),
            shape((height * width, own), F32),
        ),
        in_specs=[SMEM] + [VMEM] * (4 + len(taps[0])),
        out_specs=(VMEM,) * 3,
        scratch_shapes=[pltpu.VMEM((3 * channels, 3 * channels), BF16)]
        + [pltpu.VMEM((first_cells + 16, channels), F32)] * 3,
        compiler_params=PARAMS,
        name="first_layer",
    )(scal, mid, top, bottom, tiles, *taps[0])

    half = shape((9, own // 2, channels), F32)
    kept, sent, first_kept, first_sent, small = pl.pallas_call(
        functools.partial(last_layer, geom, scale),
        out_shape=(half, half, half, half, shape((-(-(3 * fut_here + 1) // 8) * 8, channels), F32)),
        in_specs=[SMEM] + [VMEM] * (8 + len(taps[-1])),
        out_specs=(VMEM,) * 5,
        scratch_shapes=[pltpu.VMEM((3 * channels, 3 * channels), BF16)]
        + [pltpu.VMEM((last_cells + 16, channels), F32)] * 3
        + [
            pltpu.VMEM((last_cells, channels), BF16),
            pltpu.VMEM((last_cells, channels), F32),
            pltpu.VMEM((last_cells, channels), BF16),
            pltpu.VMEM((own_cells, own), F32),
            pltpu.VMEM((3 * channels, 3 * own), BF16),
        ],
        compiler_params=PARAMS,
        name="last_layer",
    )(scal, active, slope, padded, heads_w, lines, above, below, tile, *taps[-1])

    if rows_total == 4:
        last_sum, first_sum, small = tile_sums(
            (kept, sent), (first_kept, first_sent), small, core, row_at
        )
    else:
        last_sum, first_sum, small = lax.psum(
            (
                ordered(core == 1, kept, sent, 1),
                ordered(core == 1, first_kept, first_sent, 1),
                small,
            ),
            ("rows", "cols"),
        )
    trunk_grad = jnp.stack([first_sum, last_sum])
    head_grad = small[: 3 * fut_here].reshape(fut_here, 3, channels)
    total = small[3 * fut_here, :1] / cell_count
    return (total, trunk_grad, head_grad)


def solution(mesh):
    placed = (
        P("futures", ("groups", "rows"), "cols"),
        P(None, None, "futures", None),
        P(),
        P(None, ("groups", "rows"), "cols"),
        P(("groups", "rows"), "cols"),
        P(("groups", "rows"), "cols"),
    )
    return jax.shard_map(
        local,
        mesh=mesh,
        in_specs=placed,
        out_specs=(P("groups"), P("groups", None, "futures", None), P("futures", "groups", None)),
        check_vma=False,
    )
```

```python
import functools
import math

import jax
import jax.numpy as jnp
from jax import lax
from jax.experimental import pallas as pl
from jax.experimental.pallas import tpu as pltpu
from jax.sharding import PartitionSpec as P

BLK = 8
SLOT = 16
CHUNKS = (5, 4, 5, 4)
F32 = jnp.float32
BF16 = jnp.bfloat16
VMEM = pl.BlockSpec(memory_space=pltpu.VMEM)
SMEM = pl.BlockSpec(memory_space=pltpu.SMEM)
PARAMS = pltpu.CompilerParams(vmem_limit_bytes=14 * 1024 * 1024)


def swap(block, axis, distance=1):
    count = lax.axis_size(axis)
    return lax.ppermute(block, axis, [(i, i ^ distance) for i in range(count)])


def shift(block, axis, step):
    count = lax.axis_size(axis)
    pairs = [(i, i + step) for i in range(count) if 0 <= i + step < count]
    return lax.ppermute(block, axis, pairs)


def ordered(flag, first, second, axis):
    return jnp.concatenate(
        [jnp.where(flag, second, first), jnp.where(flag, first, second)], axis=axis
    )


def pieces(total, step):
    return [(lo, min(step, total - lo)) for lo in range(0, total, step)]


def forward_tap(tap, scal, refs):
    if len(refs) == 1:
        return refs[0][tap].T
    own_ref, got_ref, mate_ref = refs
    theirs = ordered(scal[1] == 1, got_ref[tap], mate_ref[tap], 0)
    return ordered(scal[0] == 1, own_ref[tap], theirs, 1)


def forward_taps(scal, refs, mat_ref):
    for tap in range(9):
        row, col = tap // 3, tap % 3
        block = forward_tap(tap, scal, refs)
        channels = block.shape[0]
        mat_ref[
            row * channels : (row + 1) * channels, col * channels : (col + 1) * channels
        ] = block


def own_rows(value, index, count):
    size = value.shape[0] // count
    result = value[:size]
    for part in range(1, count):
        result = jnp.where(index == part, value[part * size : (part + 1) * size], result)
    return result


def clear_ends(low_ref, high_ref, count):
    blank = jnp.zeros((8, low_ref.shape[1]), F32)
    low_ref[:8, :] = blank
    high_ref[8 + count : 16 + count, :] = blank


def row_groups(count, size):
    return [(lo, min(lo + size, count)) for lo in range(0, count, size)]


def convolve(src_ref, mat_ref, low_ref, mid_ref, high_ref, rows, group, stride, finish):
    channels = src_ref.shape[1]
    clear_ends(low_ref, high_ref, SLOT + rows * stride)
    waiting = None
    for first, last in row_groups(rows, group):
        lo = SLOT + first * stride if first else 0
        hi = SLOT + last * stride
        window = jnp.concatenate(
            [src_ref[lo + row * stride : hi + row * stride, :] for row in range(3)], axis=1
        )
        width = mat_ref.shape[1] // 3
        part = jnp.dot(window, mat_ref[...], preferred_element_type=F32)
        for col, ref in enumerate((low_ref, mid_ref, high_ref)):
            ref[8 + lo : 8 + hi, :width] = part[:, col * width : (col + 1) * width]
        if waiting is not None:
            finish(*waiting)
        waiting = (first, last)
    finish(*waiting)


def combined(low_ref, mid_ref, high_ref, lo, size):
    return (
        low_ref[7 + lo : 7 + lo + size, :]
        + mid_ref[8 + lo : 8 + lo + size, :]
        + high_ref[9 + lo : 9 + lo + size, :]
    )


def own_part(value, index, count):
    width = value.shape[1] // count
    result = value[:, :width]
    for part in range(1, count):
        result = jnp.where(index == part, value[:, part * width : (part + 1) * width], result)
    return result


def chunk_of(index):
    for chunk, size in enumerate(CHUNKS):
        if index < size:
            return chunk, index
        index -= size


def kernel_grads(core, grad_ref, src_ref, base, stride, before, kept, sent):
    own = grad_ref.shape[1]
    cells = grad_ref.shape[0]
    turned = grad_ref[...].T
    moved = jnp.concatenate(
        [
            pltpu.roll(turned, cells - 1, 1).astype(BF16),
            turned.astype(BF16),
            pltpu.roll(turned, 1, 1).astype(BF16),
        ],
        axis=0,
    )
    for row in range(3):
        start = base + row * stride
        part = jnp.dot(moved, src_ref[start : start + cells, :], preferred_element_type=F32)
        for col in range(3):
            tap = 3 * row + col
            half = own // 2
            low = part[col * own : col * own + half, :]
            high = part[col * own + half : (col + 1) * own, :]
            chunk, at = chunk_of(before + tap)
            rows = slice(at * half, (at + 1) * half)
            kept[chunk][rows, :] = jnp.where(core == 1, high, low)
            sent[chunk][rows, :] = jnp.where(core == 1, low, high)


def prepare(scal, labels_in, flow_in, winner_in, taps_in, lines, *refs):
    labels, flow, winner, taps, sems = refs[-5:]
    copies = [
        pltpu.make_async_copy(source, target, sems.at[index])
        for index, (source, target) in enumerate(
            ((labels_in, labels), (flow_in, flow), (winner_in, winner), (taps_in, taps))
        )
    ]
    for copy in copies:
        copy.start()
    for copy in copies[:3]:
        copy.wait()
    height, width = labels.shape
    blocks = winner.shape[1]
    at = lax.broadcasted_iota(jnp.int32, (blocks, width), 1)
    block = lax.broadcasted_iota(jnp.int32, (blocks, width), 0)
    spread = ((at >= block * BLK) & (at < block * BLK + BLK)).astype(BF16)
    fields = [labels[...].astype(F32)]
    ids = [
        jnp.dot(winner[row : row + 1, :].astype(F32).astype(BF16), spread, preferred_element_type=F32)
        for row in range(height // BLK)
    ]
    fields.append(jnp.concatenate([jnp.broadcast_to(part, (BLK, width)) for part in ids], axis=0))
    for index in range(2):
        rest = flow[index]
        for _ in range(3):
            piece = rest.astype(BF16).astype(F32)
            fields.append(piece)
            rest = rest - piece
    for row in range(height):
        lines[row] = jnp.concatenate([field[row : row + 1] for field in fields], axis=0).astype(BF16)
    copies[3].wait()
    layers = taps.shape[0]
    turned, sends = refs[:layers], refs[layers:-5]
    for layer in range(layers):
        for tap in range(9):
            block = taps[layer, tap].T
            half = block.shape[0] // 2
            turned[layer][tap] = block
            if sends:
                sends[layer][tap] = jnp.where(scal[1] == 0, block[:half], block[half:])


def first_layer(geom, scal, mid, top, bottom, tiles, *refs):
    taps = refs[:-7]
    padded, active, slope, mat, low, cen, high = refs[-7:]
    height, width, futs, layers = geom
    stride = width + SLOT
    halo = layers + 1
    col = scal[1]
    row_at = scal[2]
    row_count = scal[3]
    slots = height + 2 * halo
    lane = lax.broadcasted_iota(jnp.int32, tiles.shape[1:], 0)
    near = (lane < SLOT // 2).astype(jnp.int32) != col
    blank = jnp.zeros(tiles.shape[1:], BF16)
    padded[:SLOT, :] = jnp.where(near & (col == 1), tiles[0], blank)
    for row in range(slots):
        at = SLOT + row * stride
        if row < halo:
            source = top[row * width : (row + 1) * width, :]
        elif row < halo + height:
            source = mid[row - halo]
        else:
            below = (row - halo - height) * width
            source = bottom[below : below + width, :]
        padded[at : at + width, :] = source
        after = tiles[row + 1] if row + 1 < slots else blank
        padded[at + width : at + stride, :] = jnp.where(
            near, jnp.where(col == 1, after, tiles[row]), blank
        )
    forward_taps(scal, taps, mat)
    spot = lax.broadcasted_iota(jnp.int32, (stride, active.shape[1]), 0)
    inside = (spot < width) | ((col == 0) & (spot < width + SLOT // 2)) | (
        (col == 1) & (spot >= width + SLOT // 2)
    )

    bump = ((spot >= width) & (col == 1)).astype(jnp.int32)

    def finish(at, size, keep):
        pre = combined(low, cen, high, at, size)
        sigma = jax.nn.sigmoid(pre)
        active[at : at + size, :] = jnp.where(keep, pre * sigma, 0.0).astype(BF16)
        return pre, sigma

    edge = halo - 1

    def finish_rows(begin, end):
        if begin == 0:
            finish(0, SLOT, (col == 1) & (row_at * height - edge >= 0))
        for row in range(begin, end):
            at = SLOT + row * stride
            place = row_at * height + row - edge
            keep = inside & (bump + place >= 0) & (bump + place < row_count * height)
            pre, sigma = finish(at, stride, keep)
            if edge <= row < edge + height:
                mine = (row - edge) * width
                own_pre = own_part(pre[:width], scal[0], futs)
                own_sig = own_part(sigma[:width], scal[0], futs)
                slope[mine : mine + width, :] = own_sig * (1.0 + own_pre * (1.0 - own_sig))

    convolve(padded, mat, low, cen, high, height + 2 * edge, 3, stride, finish_rows)


def cell_data(scal, lines, above, below, tile, height, width):
    stride = width + SLOT
    count = height + 2
    core, row_at, row_count = scal[1], scal[2], scal[3]
    beside = [block[block.shape[0] - 8 :, :width] for block in (above, below)]
    rows = beside[:1] + [lines[row] for row in range(height)] + beside[1:]
    blank = jnp.zeros(tile.shape[1:], F32)
    tiles = [blank] + [tile[row].astype(F32) for row in range(count)] + [blank]
    parts = []
    for row in range(count + 1):
        parts.append(jnp.where(core == 1, tiles[row + 1], tiles[row]))
        if row < count:
            parts.append(rows[row].astype(F32))
    flat = jnp.concatenate(parts, axis=1)
    place = lax.broadcasted_iota(jnp.int32, (8, flat.shape[1]), 1)
    line = jnp.full_like(place, -2)
    spot = place
    for row in range(count + 1):
        begin = row * stride
        line = jnp.where(place >= begin, row - 1, line)
        spot = jnp.where(place >= begin, place - (begin + SLOT), spot)
    main = spot >= 0
    right = (spot == -SLOT) & (core == 0)
    left = (spot == -1) & (core == 1)
    own = main & (line >= 0) & (line < height)
    line = line - right.astype(jnp.int32)
    at = row_at * height + line
    real = (at >= 0) & (at < row_count * height) & (line >= -1) & (line <= height)
    valid = real & (main | right | left)
    return (
        flat[0:1],
        flat[2:3] + flat[3:4] + flat[4:5],
        flat[5:6] + flat[6:7] + flat[7:8],
        flat[1:2],
        jnp.where(valid, 1.0, 0.0)[:1],
        jnp.where(own, 1.0, 0.0)[:1],
    )


def last_layer(
    geom, scale, scal, active, slope, padded, heads_w, lines, above, below, tile, *refs
):
    count = len(CHUNKS)
    taps, outs = refs[: -(10 + 2 * count)], refs[-(10 + 2 * count) : -9]
    kept, sent, small = outs[:count], outs[count:-1], outs[-1]
    mat, low, cen, high, out, bend, grad, own_grad, back_mat = refs[-9:]
    height, width, futs, layers = geom
    stride = width + SLOT
    count = grad.shape[0]
    forward_taps(scal, taps, mat)

    def finish_rows(begin, end):
        lo = SLOT + begin * stride if begin else 0
        for at, size in pieces(SLOT + end * stride - lo, stride):
            at += lo
            pre = combined(low, cen, high, at, size)
            sigma = jax.nn.sigmoid(pre)
            bend[at : at + size, :] = sigma * (1.0 + pre * (1.0 - sigma))
            out[at : at + size, :] = (pre * sigma).astype(BF16)

    convolve(active, mat, low, cen, high, height + 2, 4, stride, finish_rows)
    nfut = heads_w.shape[0] // 3
    heads = lax.dot_general(
        heads_w[...], out[...], (((1,), (1,)), ((), ())), preferred_element_type=F32
    )
    logit = heads[:nfut]
    target, flow_one, flow_two, picks, valid, own = cell_data(
        scal, lines, above, below, tile, height, width
    )
    first = heads[nfut : 2 * nfut] - flow_one
    second = heads[2 * nfut :] - flow_two
    future = lax.broadcasted_iota(jnp.int32, logit.shape, 0).astype(F32)
    mask = jnp.where(picks == future, valid, 0.0)
    cell = (
        jnp.maximum(logit, 0.0)
        + jnp.log1p(jnp.exp(-jnp.abs(logit)))
        - target * logit
        + 0.5 * (first * first + second * second)
    )
    loss = jnp.sum(jnp.where(mask * own > 0.0, cell, 0.0))
    picked = mask > 0.0
    grads = jnp.concatenate(
        [
            jnp.where(picked, (jax.nn.sigmoid(logit) - target) * scale, 0.0),
            jnp.where(picked, first * scale, 0.0),
            jnp.where(picked, second * scale, 0.0),
        ],
        axis=0,
    )
    mine = jnp.where(own > 0.0, grads, 0.0).astype(BF16)
    grads = grads.astype(BF16)
    by_head = jnp.dot(mine, out[...], preferred_element_type=F32)
    fut_here = nfut // futs
    lines = []
    for index in range(fut_here):
        for kind in range(3):
            at = kind * nfut + index
            line = by_head[at : at + 1, :]
            for part in range(1, futs):
                other = at + part * fut_here
                line = jnp.where(scal[0] == part, by_head[other : other + 1, :], line)
            lines.append(line)
    lines.append(jnp.broadcast_to(loss, (small.shape[0] - len(lines), small.shape[1])))
    totals = jnp.concatenate(lines, axis=0)
    small[...] = totals
    sent[0][kept[0].shape[0] :, :] = totals
    up = lax.dot_general(
        grads, heads_w[...], (((0,), (0,)), ((), ())), preferred_element_type=F32
    )
    low[: count, :] = up
    own_grad[...] = jnp.zeros_like(own_grad)

    def back(lo, size):
        value = (low[lo : lo + size, :] * bend[lo : lo + size, :]).astype(BF16)
        grad[lo : lo + size, :] = value
        return value

    back(0, SLOT)
    for row in range(height + 2):
        at = SLOT + row * stride
        value = back(at, stride)
        if 1 <= row <= height:
            mine_at = SLOT + (row - 1) * stride
            own_grad[mine_at : mine_at + width, :] = own_part(
                value[:width].astype(F32), scal[0], futs
            )
    kernel_grads(scal[1], own_grad, active, stride, stride, 0, kept, sent)
    back_layer(
        geom, scal, grad, taps, slope, padded, kept, sent, back_mat, low, cen, high,
        own_grad,
    )


def back_layer(
    geom, scal, grad, taps, slope, padded, kept, sent, mat, low, cen, high, own_grad
):
    height, width, futs, layers = geom
    stride = width + SLOT
    channels = grad.shape[1]
    own = channels // futs
    for tap in range(9):
        row, col = tap // 3, tap % 3
        mat[
            (2 - row) * channels : (3 - row) * channels, (2 - col) * own : (3 - col) * own
        ] = own_rows(forward_tap(tap, scal, taps), scal[0], futs).T
    own_grad[...] = jnp.zeros_like(own_grad)

    def finish_rows(begin, end):
        for row in range(begin, end):
            at = SLOT + row * stride
            up = (
                low[7 + at : 7 + at + width, :own]
                + cen[8 + at : 8 + at + width, :own]
                + high[9 + at : 9 + at + width, :own]
            )
            value = (up * slope[row * width : (row + 1) * width, :]).astype(BF16)
            own_grad[at : at + width, :] = value.astype(F32)

    convolve(grad, mat, low, cen, high, height, 4, stride, finish_rows)
    kernel_grads(scal[1], own_grad, padded, layers * stride, stride, 9, kept, sent)


def tap_parts(mine, got, after=None):
    if after is not None:
        got, _ = tied(got, after)
    return (mine, got, swap(got, "cols"))


def tied(*blocks):
    return lax.optimization_barrier(blocks)


def in_order(arrived, ready):
    return [
        tied(block, ready[index + 1])[0] if index + 1 < len(arrived) else block
        for index, block in enumerate(arrived)
    ]


def one_by_one(blocks, axis):
    arrived = []
    for block in blocks:
        if arrived:
            block = tied(block, arrived[-1])[0]
        arrived.append(swap(block, axis))
    return arrived


def split3(value):
    high = rounded(value)
    rest = value - high
    mid = rounded(rest)
    return [high.astype(BF16), mid.astype(BF16), rounded(rest - mid).astype(BF16)]


def joined(block, small):
    return jnp.concatenate([block.reshape(-1, block.shape[-1]), *split3(small)], axis=0)


def parted(block, like, small):
    size = block.shape[0] - 3 * small.shape[0]
    parts = block[size:].astype(F32).reshape(3, *small.shape)
    return block[:size].reshape(like.shape), small + (parts[0] + parts[1] + parts[2])


def tile_sums(kept, sent, small, core, row_at, half):
    bit = row_at & 1
    channels = small.shape[1]
    got = [swap(block, "cols") for block in sent]
    size = kept[0].shape[0]
    small = small + got[0][size:]
    got[0] = got[0][:size]
    blocks = [(mine + more).reshape(-1, half, channels) for mine, more in zip(kept, got)]
    half = half // 2
    kept = [jnp.where(bit == 1, block[:, half:], block[:, :half]) for block in blocks]
    sent = [jnp.where(bit == 1, block[:, :half], block[:, half:]) for block in blocks]
    ready = [rounded(block).astype(BF16) for block in sent]
    ready[0] = joined(ready[0], small)
    got = in_order([swap(block, "rows") for block in ready], ready)
    got[0], small = parted(got[0], kept[0], small)
    pairs = [rounded(mine + more.astype(F32)) for mine, more in zip(kept, got)]
    ready = [block.astype(BF16) for block in pairs]
    ready[0] = joined(ready[0], small)
    got = in_order([swap(block, "rows", 2) for block in ready], ready)
    got[0], small = parted(got[0], pairs[0], small)
    ready = [(mine + more.astype(F32)).astype(BF16) for mine, more in zip(pairs, got)]
    got = in_order([swap(block, "rows") for block in ready], ready)
    ready[-1], small = tied(ready[-1], small)
    ready = [ordered(bit == 1, mine, more, 1) for mine, more in zip(ready, got)]
    got = in_order([swap(block, "cols") for block in ready], ready)
    return [ordered(core == 1, mine, more, 1) for mine, more in zip(ready, got)], small


def rounded(value):
    return lax.reduce_precision(value, 8, 7)


def local(features, trunk_weights, head_weights, flow_target, labels, winner):
    own, height, width = features.shape
    layers, _, _, channels = trunk_weights.shape
    fut_total = head_weights.shape[0]
    futs = lax.axis_size("futures")
    fut_here = fut_total // futs
    rows_total = lax.axis_size("rows")
    fut = lax.axis_index("futures")
    core = lax.axis_index("cols")
    row_at = lax.axis_index("rows")
    cell_count = height * width * rows_total * lax.axis_size("cols")
    scale = 1.0 / math.sqrt(cell_count)
    halo = layers + 1
    stride = width + SLOT
    geom = (height, width, futs, layers)
    scal = jnp.stack([fut, core, row_at, jnp.int32(rows_total)]).astype(jnp.int32)

    shape = jax.ShapeDtypeStruct
    mine = jnp.transpose(features, (1, 2, 0))
    half_taps = shape((9, channels // 2, own), BF16)
    lines, *turned = pl.pallas_call(
        prepare,
        out_shape=(shape((height, 8, width), BF16),)
        + (shape((9, channels, own), BF16),) * layers
        + ((half_taps,) * layers if futs == 2 else ()),
        in_specs=[SMEM] + [pl.BlockSpec(memory_space=pltpu.HBM)] * 4,
        out_specs=(VMEM,) * (1 + layers + (layers if futs == 2 else 0)),
        scratch_shapes=[
            pltpu.VMEM(labels.shape, labels.dtype),
            pltpu.VMEM(flow_target.shape, F32),
            pltpu.VMEM(winner.shape, winner.dtype),
            pltpu.VMEM(trunk_weights.shape, BF16),
            pltpu.SemaphoreType.DMA((4,)),
        ],
        compiler_params=PARAMS,
        name="prepare",
    )(
        scal,
        *[
            pltpu.with_memory_space_constraint(array, pltpu.HBM)
            for array in (labels, flow_target, winner, trunk_weights)
        ],
    )
    if futs == 2:
        outer = jnp.concatenate([mine[:halo], mine[-halo:]], axis=0)
        theirs = swap(outer, "futures")
        outer = ordered(fut == 1, outer, theirs, 2)
        sends = tied(theirs, *turned[layers + 1 :])[1:]
        inner = tied(mine[halo:-halo], lines)[0]
        inner_theirs = swap(inner, "futures")
        first, last = outer[:halo], outer[halo:]
        got_taps = [swap(send, "futures") for send in [turned[layers], *sends]]
        taps = tap_parts(turned[0], got_taps[0])
    else:
        mid = lax.all_gather(mine, "futures", axis=2, tiled=True)
        first, last = mid[:halo], mid[-halo:]
        whole_taps = lax.all_gather(trunk_weights, "futures", axis=2, tiled=True)
        taps = (whole_taps[0],)

    def with_line(block, line):
        line = jnp.pad(line, ((0, 0), (0, channels - width)))
        return jnp.concatenate([block.reshape(-1, channels), line], axis=0)

    top = shift(with_line(last, lines[-1]), "rows", 1)
    bottom = shift(with_line(first, lines[0]), "rows", -1)
    if futs == 2:
        top, bottom, inner_theirs = tied(top, bottom, inner_theirs)
        inner = ordered(fut == 1, inner, inner_theirs, 2)
        mid = jnp.concatenate([first, inner, last], axis=0)

    def halo_rows(block):
        return block[: halo * width].reshape(halo, width, channels)

    def line_of(block):
        return block[halo * width :, :width]

    def edge_of(block):
        return jnp.where(core == 0, block[..., -SLOT:, :], block[..., :SLOT, :])

    tiles = swap(
        jnp.concatenate([edge_of(halo_rows(top)), edge_of(mid), edge_of(halo_rows(bottom))], axis=0), "cols"
    )
    line_rows = jnp.concatenate([line_of(top)[None], lines, line_of(bottom)[None]], axis=0)
    tile = swap(
        jnp.where(core == 0, line_rows[:, :, -SLOT:], line_rows[:, :, :SLOT]), "cols"
    )
    heads_w = jnp.transpose(head_weights, (1, 0, 2)).reshape(3 * fut_total, channels)

    def cells(rows):
        return SLOT + rows * stride

    first_cells = cells(height + 4)
    last_cells = cells(height + 2)
    own_cells = -(-cells(height) // 128) * 128
    padded, active, slope = pl.pallas_call(
        functools.partial(first_layer, geom),
        out_shape=(
            shape((cells(height + 6), channels), BF16),
            shape((first_cells, channels), BF16),
            shape((height * width, own), F32),
        ),
        in_specs=[SMEM] + [VMEM] * (4 + len(taps)),
        out_specs=(VMEM,) * 3,
        scratch_shapes=[pltpu.VMEM((3 * channels, 3 * channels), BF16)]
        + [pltpu.VMEM((first_cells + 16, channels), F32)] * 3,
        compiler_params=PARAMS,
        name="first_layer",
    )(scal, mid, top, bottom, tiles, *taps)

    if futs == 2:
        taps = tap_parts(turned[layers - 1], got_taps[layers - 1], active)
    else:
        taps = (whole_taps[layers - 1],)
    lines_out = -(-(3 * fut_here + 1) // 8) * 8
    sizes = [size * (own // 2) for size in CHUNKS]
    kept_out = tuple(shape((size, channels), F32) for size in sizes)
    sizes[0] += lines_out
    sent_out = tuple(shape((size, channels), F32) for size in sizes)
    *parts, small = pl.pallas_call(
        functools.partial(last_layer, geom, scale),
        out_shape=kept_out + sent_out + (shape((lines_out, channels), F32),),
        in_specs=[SMEM] + [VMEM] * (8 + len(taps)),
        out_specs=(VMEM,) * (2 * len(CHUNKS) + 1),
        scratch_shapes=[pltpu.VMEM((3 * channels, 3 * channels), BF16)]
        + [pltpu.VMEM((last_cells + 16, channels), F32)] * 3
        + [
            pltpu.VMEM((last_cells, channels), BF16),
            pltpu.VMEM((last_cells, channels), F32),
            pltpu.VMEM((last_cells, channels), BF16),
            pltpu.VMEM((own_cells, own), F32),
            pltpu.VMEM((3 * channels, 3 * own), BF16),
        ],
        compiler_params=PARAMS,
        name="last_layer",
    )(scal, active, slope, padded, heads_w, lines, top, bottom, tile, *taps)

    kept, sent = parts[: len(CHUNKS)], parts[len(CHUNKS) :]
    if rows_total == 4:
        sums, small = tile_sums(kept, sent, small, core, row_at, own // 2)
    else:
        sent[0] = sent[0][:-lines_out]
        sums = [
            ordered(core == 1, *[part.reshape(-1, own // 2, channels) for part in both], 1)
            for both in zip(kept, sent)
        ]
        sums, small = lax.psum((sums, small), ("rows", "cols"))
    taps_of = []
    for layer in range(layers):
        low = 9 * (layers - 1 - layer)
        begin = 0
        for block in sums:
            first = max(low - begin, 0)
            last = min(low + 9 - begin, block.shape[0])
            if first < last:
                taps_of.append(block[first:last])
            begin += block.shape[0]
    trunk_grad = jnp.concatenate(taps_of, axis=0).astype(F32).reshape(layers, 9, own, channels)
    head_grad = small[: 3 * fut_here].reshape(fut_here, 3, channels)
    total = small[3 * fut_here, :1] / cell_count
    return (total, trunk_grad, head_grad)


def solution(mesh):
    placed = (
        P("futures", ("groups", "rows"), "cols"),
        P(None, None, "futures", None),
        P(),
        P(None, ("groups", "rows"), "cols"),
        P(("groups", "rows"), "cols"),
        P(("groups", "rows"), "cols"),
    )
    return jax.shard_map(
        local,
        mesh=mesh,
        in_specs=placed,
        out_specs=(P("groups"), P("groups", None, "futures", None), P("futures", "groups", None)),
        check_vma=False,
    )
```

```python
import functools
import math

import jax
import jax.numpy as jnp
from jax import lax
from jax.experimental import pallas as pl
from jax.experimental.pallas import tpu as pltpu
from jax.sharding import PartitionSpec as P

BLK = 8
SLOT = 16
CHUNKS = (5, 4, 5, 4)
F32 = jnp.float32
BF16 = jnp.bfloat16
VMEM = pl.BlockSpec(memory_space=pltpu.VMEM)
SMEM = pl.BlockSpec(memory_space=pltpu.SMEM)


def limited(mebibytes):
    return pltpu.CompilerParams(vmem_limit_bytes=mebibytes * 1024 * 1024)


def swap(block, axis, distance=1):
    count = lax.axis_size(axis)
    return lax.ppermute(block, axis, [(i, i ^ distance) for i in range(count)])


def shift(block, axis, step):
    count = lax.axis_size(axis)
    pairs = [(i, i + step) for i in range(count) if 0 <= i + step < count]
    return lax.ppermute(block, axis, pairs)


def ordered(flag, first, second, axis):
    return jnp.concatenate(
        [jnp.where(flag, second, first), jnp.where(flag, first, second)], axis=axis
    )


def pieces(total, step):
    return [(lo, min(step, total - lo)) for lo in range(0, total, step)]


def forward_tap(tap, scal, refs):
    if len(refs) == 1:
        return refs[0][tap].T
    own_ref, got_ref, mate_ref = refs
    theirs = ordered(scal[1] == 1, got_ref[tap], mate_ref[tap], 0)
    return ordered(scal[0] == 1, own_ref[tap], theirs, 1)


def forward_taps(scal, refs, mat_ref):
    for tap in range(9):
        row, col = tap // 3, tap % 3
        block = forward_tap(tap, scal, refs)
        channels = block.shape[0]
        mat_ref[
            row * channels : (row + 1) * channels, col * channels : (col + 1) * channels
        ] = block


def own_rows(value, index, count):
    size = value.shape[0] // count
    result = value[:size]
    for part in range(1, count):
        result = jnp.where(index == part, value[part * size : (part + 1) * size], result)
    return result


def clear_ends(low_ref, high_ref, count):
    blank = jnp.zeros((8, low_ref.shape[1]), F32)
    low_ref[:8, :] = blank
    high_ref[8 + count : 16 + count, :] = blank


def row_groups(count, size):
    return [(lo, min(lo + size, count)) for lo in range(0, count, size)]


def convolve(src_ref, mat_ref, low_ref, mid_ref, high_ref, rows, group, stride, finish):
    channels = src_ref.shape[1]
    clear_ends(low_ref, high_ref, SLOT + rows * stride)
    waiting = None
    for first, last in row_groups(rows, group):
        lo = SLOT + first * stride if first else 0
        hi = SLOT + last * stride
        window = jnp.concatenate(
            [src_ref[lo + row * stride : hi + row * stride, :] for row in range(3)], axis=1
        )
        width = mat_ref.shape[1] // 3
        part = jnp.dot(window, mat_ref[...], preferred_element_type=F32)
        for col, ref in enumerate((low_ref, mid_ref, high_ref)):
            ref[8 + lo : 8 + hi, :width] = part[:, col * width : (col + 1) * width]
        if waiting is not None:
            finish(*waiting)
        waiting = (first, last)
    finish(*waiting)


def combined(low_ref, mid_ref, high_ref, lo, size):
    return (
        low_ref[7 + lo : 7 + lo + size, :]
        + mid_ref[8 + lo : 8 + lo + size, :]
        + high_ref[9 + lo : 9 + lo + size, :]
    )


def own_part(value, index, count):
    width = value.shape[1] // count
    result = value[:, :width]
    for part in range(1, count):
        result = jnp.where(index == part, value[:, part * width : (part + 1) * width], result)
    return result


def chunk_of(index):
    for chunk, size in enumerate(CHUNKS):
        if index < size:
            return chunk, index
        index -= size


def kernel_grads(core, grad_ref, src_ref, base, stride, before, kept, sent):
    own = grad_ref.shape[1]
    cells = grad_ref.shape[0]
    turned = grad_ref[...].T.astype(BF16)
    moved = jnp.concatenate(
        [
            pltpu.roll(turned, cells - 1, 1),
            turned,
            pltpu.roll(turned, 1, 1),
        ],
        axis=0,
    )
    for row in range(3):
        start = base + row * stride
        part = jnp.dot(moved, src_ref[start : start + cells, :], preferred_element_type=F32)
        for col in range(3):
            tap = 3 * row + col
            half = own // 2
            low = part[col * own : col * own + half, :]
            high = part[col * own + half : (col + 1) * own, :]
            chunk, at = chunk_of(before + tap)
            rows = slice(at * half, (at + 1) * half)
            kept[chunk][rows, :] = jnp.where(core == 1, high, low)
            sent[chunk][rows, :] = jnp.where(core == 1, low, high)


def prepare(scal, labels_in, flow_in, winner_in, taps_in, lines, *refs):
    labels, flow, winner, taps, sems = refs[-5:]
    copies = [
        pltpu.make_async_copy(source, target, sems.at[index])
        for index, (source, target) in enumerate(
            ((labels_in, labels), (flow_in, flow), (winner_in, winner), (taps_in, taps))
        )
    ]
    for copy in copies:
        copy.start()
    for copy in copies[:3]:
        copy.wait()
    height, width = labels.shape
    blocks = winner.shape[1]
    at = lax.broadcasted_iota(jnp.int32, (blocks, width), 1)
    block = lax.broadcasted_iota(jnp.int32, (blocks, width), 0)
    spread = ((at >= block * BLK) & (at < block * BLK + BLK)).astype(BF16)
    fields = [labels[...].astype(F32)]
    ids = [
        jnp.dot(winner[row : row + 1, :].astype(F32).astype(BF16), spread, preferred_element_type=F32)
        for row in range(height // BLK)
    ]
    fields.append(jnp.concatenate([jnp.broadcast_to(part, (BLK, width)) for part in ids], axis=0))
    for index in range(2):
        rest = flow[index]
        for _ in range(3):
            piece = rest.astype(BF16).astype(F32)
            fields.append(piece)
            rest = rest - piece
    for row in range(height):
        lines[row] = jnp.concatenate([field[row : row + 1] for field in fields], axis=0).astype(BF16)
    copies[3].wait()
    layers = taps.shape[0]
    turned, sends = refs[:layers], refs[layers:-5]
    for layer in range(layers):
        for tap in range(9):
            block = taps[layer, tap].T
            half = block.shape[0] // 2
            turned[layer][tap] = block
            if sends:
                sends[layer][tap] = jnp.where(scal[1] == 0, block[:half], block[half:])


def first_layer(geom, scal, mid, top, bottom, tiles, *refs):
    taps = refs[:-7]
    padded, active, slope, mat, low, cen, high = refs[-7:]
    height, width, futs, layers = geom
    stride = width + SLOT
    halo = layers + 1
    col = scal[1]
    row_at = scal[2]
    row_count = scal[3]
    slots = height + 2 * halo
    tiles = [tiles[row * SLOT : (row + 1) * SLOT, :] for row in range(slots)]
    lane = lax.broadcasted_iota(jnp.int32, tiles[0].shape, 0)
    near = (lane < SLOT // 2).astype(jnp.int32) != col
    blank = jnp.zeros(tiles[0].shape, BF16)
    padded[:SLOT, :] = jnp.where(near & (col == 1), tiles[0], blank)
    for row in range(slots):
        at = SLOT + row * stride
        if row < halo:
            source = top[row * width : (row + 1) * width, :]
        elif row < halo + height:
            source = mid[row - halo]
        else:
            below = (row - halo - height) * width
            source = bottom[below : below + width, :]
        padded[at : at + width, :] = source
        after = tiles[row + 1] if row + 1 < slots else blank
        padded[at + width : at + stride, :] = jnp.where(
            near, jnp.where(col == 1, after, tiles[row]), blank
        )
    forward_taps(scal, taps, mat)
    spot = lax.broadcasted_iota(jnp.int32, (stride, active.shape[1]), 0)
    inside = (spot < width) | ((col == 0) & (spot < width + SLOT // 2)) | (
        (col == 1) & (spot >= width + SLOT // 2)
    )

    bump = ((spot >= width) & (col == 1)).astype(jnp.int32)

    def finish(at, size, keep):
        pre = combined(low, cen, high, at, size)
        sigma = jax.nn.sigmoid(pre)
        active[at : at + size, :] = jnp.where(keep, pre * sigma, 0.0).astype(BF16)
        return pre, sigma

    edge = halo - 1

    def finish_rows(begin, end):
        if begin == 0:
            finish(0, SLOT, (col == 1) & (row_at * height - edge >= 0))
        for row in range(begin, end):
            at = SLOT + row * stride
            place = row_at * height + row - edge
            keep = inside & (bump + place >= 0) & (bump + place < row_count * height)
            pre, sigma = finish(at, stride, keep)
            if edge <= row < edge + height:
                mine = (row - edge) * width
                own_pre = own_part(pre[:width], scal[0], futs)
                own_sig = own_part(sigma[:width], scal[0], futs)
                slope[mine : mine + width, :] = own_sig * (1.0 + own_pre * (1.0 - own_sig))

    convolve(padded, mat, low, cen, high, height + 2 * edge, 3, stride, finish_rows)


def cell_data(scal, lines, above, below, tile, height, width):
    stride = width + SLOT
    count = height + 2
    core, row_at, row_count = scal[1], scal[2], scal[3]
    beside = [block[block.shape[0] - 8 :, :width] for block in (above, below)]
    rows = beside[:1] + [lines[row] for row in range(height)] + beside[1:]
    blank = jnp.zeros((8, SLOT), F32)
    begin = tile.shape[0] - 8 * count
    tiles = [tile[begin + 8 * row : begin + 8 * row + 8, :SLOT].astype(F32) for row in range(count)]
    tiles = [blank, *tiles, blank]
    parts = []
    for row in range(count + 1):
        parts.append(jnp.where(core == 1, tiles[row + 1], tiles[row]))
        if row < count:
            parts.append(rows[row].astype(F32))
    flat = jnp.concatenate(parts, axis=1)
    place = lax.broadcasted_iota(jnp.int32, (8, flat.shape[1]), 1)
    line = jnp.full_like(place, -2)
    spot = place
    for row in range(count + 1):
        begin = row * stride
        line = jnp.where(place >= begin, row - 1, line)
        spot = jnp.where(place >= begin, place - (begin + SLOT), spot)
    main = spot >= 0
    right = (spot == -SLOT) & (core == 0)
    left = (spot == -1) & (core == 1)
    own = main & (line >= 0) & (line < height)
    line = line - right.astype(jnp.int32)
    at = row_at * height + line
    real = (at >= 0) & (at < row_count * height) & (line >= -1) & (line <= height)
    valid = real & (main | right | left)
    return (
        flat[0:1],
        flat[2:3] + flat[3:4] + flat[4:5],
        flat[5:6] + flat[6:7] + flat[7:8],
        flat[1:2],
        jnp.where(valid, 1.0, 0.0)[:1],
        jnp.where(own, 1.0, 0.0)[:1],
    )


def last_layer(
    geom, scale, scal, active, slope, padded, heads_w, lines, above, below, tile, *refs
):
    count = len(CHUNKS)
    taps, outs = refs[: -(10 + 2 * count)], refs[-(10 + 2 * count) : -9]
    kept, sent, small = outs[:count], outs[count:-1], outs[-1]
    mat, low, cen, high, out, bend, grad, own_grad, back_mat = refs[-9:]
    height, width, futs, layers = geom
    stride = width + SLOT
    count = grad.shape[0]
    forward_taps(scal, taps, mat)

    def finish_rows(begin, end):
        lo = SLOT + begin * stride if begin else 0
        for at, size in pieces(SLOT + end * stride - lo, stride):
            at += lo
            pre = combined(low, cen, high, at, size)
            sigma = jax.nn.sigmoid(pre)
            bend[at : at + size, :] = sigma * (1.0 + pre * (1.0 - sigma))
            out[at : at + size, :] = (pre * sigma).astype(BF16)

    convolve(active, mat, low, cen, high, height + 2, 4, stride, finish_rows)
    nfut = heads_w.shape[0] // 3
    heads = lax.dot_general(
        heads_w[...], out[...], (((1,), (1,)), ((), ())), preferred_element_type=F32
    )
    logit = heads[:nfut]
    target, flow_one, flow_two, picks, valid, own = cell_data(
        scal, lines, above, below, tile, height, width
    )
    first = heads[nfut : 2 * nfut] - flow_one
    second = heads[2 * nfut :] - flow_two
    future = lax.broadcasted_iota(jnp.int32, logit.shape, 0).astype(F32)
    mask = jnp.where(picks == future, valid, 0.0)
    cell = (
        jnp.maximum(logit, 0.0)
        + jnp.log1p(jnp.exp(-jnp.abs(logit)))
        - target * logit
        + 0.5 * (first * first + second * second)
    )
    loss = jnp.sum(jnp.where(mask * own > 0.0, cell, 0.0))
    picked = mask > 0.0
    grads = jnp.concatenate(
        [
            jnp.where(picked, (jax.nn.sigmoid(logit) - target) * scale, 0.0),
            jnp.where(picked, first * scale, 0.0),
            jnp.where(picked, second * scale, 0.0),
        ],
        axis=0,
    )
    mine = jnp.where(own > 0.0, grads, 0.0).astype(BF16)
    grads = grads.astype(BF16)
    by_head = jnp.dot(mine, out[...], preferred_element_type=F32)
    fut_here = nfut // futs
    lines = []
    for index in range(fut_here):
        for kind in range(3):
            at = kind * nfut + index
            line = by_head[at : at + 1, :]
            for part in range(1, futs):
                other = at + part * fut_here
                line = jnp.where(scal[0] == part, by_head[other : other + 1, :], line)
            lines.append(line)
    lines.append(jnp.broadcast_to(loss, (small.shape[0] - len(lines), small.shape[1])))
    totals = jnp.concatenate(lines, axis=0)
    small[...] = totals
    sent[0][kept[0].shape[0] :, :] = totals
    up = lax.dot_general(
        grads, heads_w[...], (((0,), (0,)), ((), ())), preferred_element_type=F32
    )
    low[: count, :] = up
    own_grad[...] = jnp.zeros_like(own_grad)

    def back(lo, size):
        value = (low[lo : lo + size, :] * bend[lo : lo + size, :]).astype(BF16)
        grad[lo : lo + size, :] = value
        return value

    back(0, SLOT)
    for row in range(height + 2):
        at = SLOT + row * stride
        value = back(at, stride)
        if 1 <= row <= height:
            mine_at = SLOT + (row - 1) * stride
            own_grad[mine_at : mine_at + width, :] = own_part(
                value[:width].astype(F32), scal[0], futs
            )
    kernel_grads(scal[1], own_grad, active, stride, stride, 0, kept, sent)
    back_layer(
        geom, scal, grad, taps, slope, padded, kept, sent, back_mat, low, cen, high,
        own_grad,
    )


def back_layer(
    geom, scal, grad, taps, slope, padded, kept, sent, mat, low, cen, high, own_grad
):
    height, width, futs, layers = geom
    stride = width + SLOT
    channels = grad.shape[1]
    own = channels // futs
    for tap in range(9):
        row, col = tap // 3, tap % 3
        mat[
            (2 - row) * channels : (3 - row) * channels, (2 - col) * own : (3 - col) * own
        ] = own_rows(forward_tap(tap, scal, taps), scal[0], futs).T
    own_grad[...] = jnp.zeros_like(own_grad)

    def finish_rows(begin, end):
        for row in range(begin, end):
            at = SLOT + row * stride
            up = (
                low[7 + at : 7 + at + width, :own]
                + cen[8 + at : 8 + at + width, :own]
                + high[9 + at : 9 + at + width, :own]
            )
            value = (up * slope[row * width : (row + 1) * width, :]).astype(BF16)
            own_grad[at : at + width, :] = value.astype(F32)

    convolve(grad, mat, low, cen, high, height, 4, stride, finish_rows)
    kernel_grads(scal[1], own_grad, padded, layers * stride, stride, 9, kept, sent)


def tap_parts(mine, got, after=None):
    if after is not None:
        got, _ = tied(got, after)
    return (mine, got, swap(got, "cols"))


def tied(*blocks):
    return lax.optimization_barrier(blocks)


def in_order(arrived, ready):
    return [
        tied(block, ready[index + 1])[0] if index + 1 < len(arrived) else block
        for index, block in enumerate(arrived)
    ]


def one_by_one(blocks, axis):
    arrived = []
    for block in blocks:
        if arrived:
            block = tied(block, arrived[-1])[0]
        arrived.append(swap(block, axis))
    return arrived


def split3(value):
    high = rounded(value)
    rest = value - high
    mid = rounded(rest)
    return [high.astype(BF16), mid.astype(BF16), rounded(rest - mid).astype(BF16)]


def joined(block, small):
    return jnp.concatenate([block.reshape(-1, block.shape[-1]), *split3(small)], axis=0)


def parted(block, like, small):
    size = block.shape[0] - 3 * small.shape[0]
    parts = block[size:].astype(F32).reshape(3, *small.shape)
    return block[:size].reshape(like.shape), small + (parts[0] + parts[1] + parts[2])


def tile_sums(kept, sent, small, core, row_at, half):
    bit = row_at & 1
    channels = small.shape[1]
    got = [swap(block, "cols") for block in sent]
    size = kept[0].shape[0]
    small = small + got[0][size:]
    got[0] = got[0][:size]
    blocks = [(mine + more).reshape(-1, half, channels) for mine, more in zip(kept, got)]
    half = half // 2
    kept = [jnp.where(bit == 1, block[:, half:], block[:, :half]) for block in blocks]
    sent = [jnp.where(bit == 1, block[:, :half], block[:, half:]) for block in blocks]
    ready = [rounded(block).astype(BF16) for block in sent]
    ready[0] = joined(ready[0], small)
    got = in_order([swap(block, "rows") for block in ready], ready)
    got[0], small = parted(got[0], kept[0], small)
    pairs = [rounded(mine + more.astype(F32)) for mine, more in zip(kept, got)]
    ready = [block.astype(BF16) for block in pairs]
    ready[0] = joined(ready[0], small)
    got = in_order([swap(block, "rows", 2) for block in ready], ready)
    got[0], small = parted(got[0], pairs[0], small)
    ready = [(mine + more.astype(F32)).astype(BF16) for mine, more in zip(pairs, got)]
    got = in_order([swap(block, "rows") for block in ready], ready)
    ready[-1], small = tied(ready[-1], small)
    ready = [ordered(bit == 1, mine, more, 1) for mine, more in zip(ready, got)]
    got = in_order([swap(block, "cols") for block in ready], ready)
    return [ordered(core == 1, mine, more, 1) for mine, more in zip(ready, got)], small


def rounded(value):
    return lax.reduce_precision(value, 8, 7)


def local(features, trunk_weights, head_weights, flow_target, labels, winner):
    own, height, width = features.shape
    layers, _, _, channels = trunk_weights.shape
    fut_total = head_weights.shape[0]
    futs = lax.axis_size("futures")
    fut_here = fut_total // futs
    rows_total = lax.axis_size("rows")
    fut = lax.axis_index("futures")
    core = lax.axis_index("cols")
    row_at = lax.axis_index("rows")
    cell_count = height * width * rows_total * lax.axis_size("cols")
    scale = 1.0 / math.sqrt(cell_count)
    halo = layers + 1
    stride = width + SLOT
    geom = (height, width, futs, layers)
    scal = jnp.stack([fut, core, row_at, jnp.int32(rows_total)]).astype(jnp.int32)

    shape = jax.ShapeDtypeStruct
    mine = jnp.transpose(features, (1, 2, 0))
    half_taps = shape((9, channels // 2, own), BF16)
    lines, *turned = pl.pallas_call(
        prepare,
        out_shape=(shape((height, 8, width), BF16),)
        + (shape((9, channels, own), BF16),) * layers
        + ((half_taps,) * layers if futs == 2 else ()),
        in_specs=[SMEM] + [pl.BlockSpec(memory_space=pltpu.HBM)] * 4,
        out_specs=(VMEM,) * (1 + layers + (layers if futs == 2 else 0)),
        scratch_shapes=[
            pltpu.VMEM(labels.shape, labels.dtype),
            pltpu.VMEM(flow_target.shape, F32),
            pltpu.VMEM(winner.shape, winner.dtype),
            pltpu.VMEM(trunk_weights.shape, BF16),
            pltpu.SemaphoreType.DMA((4,)),
        ],
        compiler_params=limited(4),
        name="prepare",
    )(
        scal,
        *[
            pltpu.with_memory_space_constraint(array, pltpu.HBM)
            for array in (labels, flow_target, winner, trunk_weights)
        ],
    )
    if futs == 2:
        outer = jnp.concatenate([mine[:halo], mine[-halo:]], axis=0)
        theirs = swap(outer, "futures")
        outer = ordered(fut == 1, outer, theirs, 2)
        sends = tied(theirs, *turned[layers + 1 :])[1:]
        inner = tied(mine[halo:-halo], lines)[0]
        inner_theirs = swap(inner, "futures")
        first, last = outer[:halo], outer[halo:]
        got_taps = [swap(send, "futures") for send in [turned[layers], *sends]]
        taps = tap_parts(turned[0], got_taps[0])
    else:
        mid = lax.all_gather(mine, "futures", axis=2, tiled=True)
        first, last = mid[:halo], mid[-halo:]
        whole_taps = lax.all_gather(trunk_weights, "futures", axis=2, tiled=True)
        taps = (whole_taps[0],)

    def with_line(block, line):
        line = jnp.pad(line, ((0, 0), (0, channels - width)))
        return jnp.concatenate([block.reshape(-1, channels), line], axis=0)

    top, bottom = tied(with_line(last, lines[-1]), with_line(first, lines[0]))
    top, bottom = shift(top, "rows", 1), shift(bottom, "rows", -1)
    if futs == 2:
        top, bottom, inner_theirs = tied(top, bottom, inner_theirs)
        inner = ordered(fut == 1, inner, inner_theirs, 2)
        mid = jnp.concatenate([first, inner, last], axis=0)

    def halo_rows(block):
        return block[: halo * width].reshape(halo, width, channels)

    def line_of(block):
        return block[halo * width :, :width]

    def edge_of(block):
        return jnp.where(core == 0, block[..., -SLOT:, :], block[..., :SLOT, :])

    line_rows = jnp.concatenate([line_of(top)[None], lines, line_of(bottom)[None]], axis=0)
    edges = jnp.where(core == 0, line_rows[:, :, -SLOT:], line_rows[:, :, :SLOT])
    edges = jnp.pad(edges.reshape(-1, SLOT), ((0, 0), (0, channels - SLOT)))
    blocks = [edge_of(halo_rows(top)), edge_of(mid), edge_of(halo_rows(bottom))]
    tiles = swap(
        jnp.concatenate([block.reshape(-1, channels) for block in blocks] + [edges], axis=0),
        "cols",
    )
    heads_w = jnp.transpose(head_weights, (1, 0, 2)).reshape(3 * fut_total, channels)

    def cells(rows):
        return SLOT + rows * stride

    first_cells = cells(height + 4)
    last_cells = cells(height + 2)
    own_cells = -(-cells(height) // 128) * 128
    padded, active, slope = pl.pallas_call(
        functools.partial(first_layer, geom),
        out_shape=(
            shape((cells(height + 6), channels), BF16),
            shape((first_cells, channels), BF16),
            shape((height * width, own), F32),
        ),
        in_specs=[SMEM] + [VMEM] * (4 + len(taps)),
        out_specs=(VMEM,) * 3,
        scratch_shapes=[pltpu.VMEM((3 * channels, 3 * channels), BF16)]
        + [pltpu.VMEM((first_cells + 16, channels), F32)] * 3,
        compiler_params=limited(8),
        name="first_layer",
    )(scal, mid, top, bottom, tiles, *taps)

    if futs == 2:
        taps = tap_parts(turned[layers - 1], got_taps[layers - 1], active)
    else:
        taps = (whole_taps[layers - 1],)
    lines_out = -(-(3 * fut_here + 1) // 8) * 8
    sizes = [size * (own // 2) for size in CHUNKS]
    kept_out = tuple(shape((size, channels), F32) for size in sizes)
    sizes[0] += lines_out
    sent_out = tuple(shape((size, channels), F32) for size in sizes)
    *parts, small = pl.pallas_call(
        functools.partial(last_layer, geom, scale),
        out_shape=kept_out + sent_out + (shape((lines_out, channels), F32),),
        in_specs=[SMEM] + [VMEM] * (8 + len(taps)),
        out_specs=(VMEM,) * (2 * len(CHUNKS) + 1),
        scratch_shapes=[pltpu.VMEM((3 * channels, 3 * channels), BF16)]
        + [pltpu.VMEM((last_cells + 16, channels), F32)] * 3
        + [
            pltpu.VMEM((last_cells, channels), BF16),
            pltpu.VMEM((last_cells, channels), F32),
            pltpu.VMEM((last_cells, channels), BF16),
            pltpu.VMEM((own_cells, own), F32),
            pltpu.VMEM((3 * channels, 3 * own), BF16),
        ],
        compiler_params=limited(12),
        name="last_layer",
    )(scal, active, slope, padded, heads_w, lines, top, bottom, tiles, *taps)

    kept, sent = parts[: len(CHUNKS)], parts[len(CHUNKS) :]
    if rows_total == 4:
        sums, small = tile_sums(kept, sent, small, core, row_at, own // 2)
    else:
        sent[0] = sent[0][:-lines_out]
        sums = [
            ordered(core == 1, *[part.reshape(-1, own // 2, channels) for part in both], 1)
            for both in zip(kept, sent)
        ]
        sums, small = lax.psum((sums, small), ("rows", "cols"))
    taps_of = []
    for layer in range(layers):
        low = 9 * (layers - 1 - layer)
        begin = 0
        for block in sums:
            first = max(low - begin, 0)
            last = min(low + 9 - begin, block.shape[0])
            if first < last:
                taps_of.append(block[first:last])
            begin += block.shape[0]
    trunk_grad = jnp.concatenate(taps_of, axis=0).astype(F32).reshape(layers, 9, own, channels)
    head_grad = small[: 3 * fut_here].reshape(fut_here, 3, channels)
    total = small[3 * fut_here, :1] / cell_count
    return (total, trunk_grad, head_grad)


def solution(mesh):
    placed = (
        P("futures", ("groups", "rows"), "cols"),
        P(None, None, "futures", None),
        P(),
        P(None, ("groups", "rows"), "cols"),
        P(("groups", "rows"), "cols"),
        P(("groups", "rows"), "cols"),
    )
    return jax.shard_map(
        local,
        mesh=mesh,
        in_specs=placed,
        out_specs=(P("groups"), P("groups", None, "futures", None), P("futures", "groups", None)),
        check_vma=False,
    )
```

```python
import functools
import math

import jax
import jax.numpy as jnp
from jax import lax
from jax.experimental import pallas as pl
from jax.experimental.pallas import tpu as pltpu
from jax.sharding import PartitionSpec as P

BLK = 8
SLOT = 16
CHUNKS = (5, 4, 5, 4)
F32 = jnp.float32
BF16 = jnp.bfloat16
VMEM = pl.BlockSpec(memory_space=pltpu.VMEM)
SMEM = pl.BlockSpec(memory_space=pltpu.SMEM)


def limited(mebibytes):
    return pltpu.CompilerParams(vmem_limit_bytes=mebibytes * 1024 * 1024)


def swap(block, axis, distance=1):
    count = lax.axis_size(axis)
    return lax.ppermute(block, axis, [(i, i ^ distance) for i in range(count)])


def shift(block, axis, step):
    count = lax.axis_size(axis)
    pairs = [(i, i + step) for i in range(count) if 0 <= i + step < count]
    return lax.ppermute(block, axis, pairs)


def ordered(flag, first, second, axis):
    return jnp.concatenate(
        [jnp.where(flag, second, first), jnp.where(flag, first, second)], axis=axis
    )


def pieces(total, step):
    return [(lo, min(step, total - lo)) for lo in range(0, total, step)]


def forward_tap(tap, scal, refs):
    if len(refs) == 1:
        return refs[0][tap].T
    own_ref, got_ref, mate_ref = refs
    theirs = ordered(scal[1] == 1, got_ref[tap], mate_ref[tap], 0)
    return ordered(scal[0] == 1, own_ref[tap], theirs, 1)


def forward_taps(scal, refs, mat_ref):
    for tap in range(9):
        row, col = tap // 3, tap % 3
        block = forward_tap(tap, scal, refs)
        channels = block.shape[0]
        mat_ref[
            row * channels : (row + 1) * channels, col * channels : (col + 1) * channels
        ] = block


def own_rows(value, index, count):
    size = value.shape[0] // count
    result = value[:size]
    for part in range(1, count):
        result = jnp.where(index == part, value[part * size : (part + 1) * size], result)
    return result


def clear_ends(low_ref, high_ref, count):
    blank = jnp.zeros((8, low_ref.shape[1]), F32)
    low_ref[:8, :] = blank
    high_ref[8 + count : 16 + count, :] = blank


def row_groups(count, size):
    return [(lo, min(lo + size, count)) for lo in range(0, count, size)]


def convolve(src_ref, mat_ref, low_ref, mid_ref, high_ref, rows, group, stride, finish):
    channels = src_ref.shape[1]
    clear_ends(low_ref, high_ref, SLOT + rows * stride)
    waiting = None
    for first, last in row_groups(rows, group):
        lo = SLOT + first * stride if first else 0
        hi = SLOT + last * stride
        window = jnp.concatenate(
            [src_ref[lo + row * stride : hi + row * stride, :] for row in range(3)], axis=1
        )
        width = mat_ref.shape[1] // 3
        part = jnp.dot(window, mat_ref[...], preferred_element_type=F32)
        for col, ref in enumerate((low_ref, mid_ref, high_ref)):
            ref[8 + lo : 8 + hi, :width] = part[:, col * width : (col + 1) * width]
        if waiting is not None:
            finish(*waiting)
        waiting = (first, last)
    finish(*waiting)


def combined(low_ref, mid_ref, high_ref, lo, size):
    return (
        low_ref[7 + lo : 7 + lo + size, :]
        + mid_ref[8 + lo : 8 + lo + size, :]
        + high_ref[9 + lo : 9 + lo + size, :]
    )


def own_part(value, index, count):
    width = value.shape[1] // count
    result = value[:, :width]
    for part in range(1, count):
        result = jnp.where(index == part, value[:, part * width : (part + 1) * width], result)
    return result


def chunk_of(index):
    for chunk, size in enumerate(CHUNKS):
        if index < size:
            return chunk, index
        index -= size


def kernel_grads(core, grad_ref, src_ref, base, stride, before, kept, sent):
    own = grad_ref.shape[1]
    cells = grad_ref.shape[0]
    turned = grad_ref[...].T.astype(BF16)
    moved = jnp.concatenate(
        [
            pltpu.roll(turned, cells - 1, 1),
            turned,
            pltpu.roll(turned, 1, 1),
        ],
        axis=0,
    )
    for row in range(3):
        start = base + row * stride
        part = jnp.dot(moved, src_ref[start : start + cells, :], preferred_element_type=F32)
        for col in range(3):
            tap = 3 * row + col
            half = own // 2
            low = part[col * own : col * own + half, :]
            high = part[col * own + half : (col + 1) * own, :]
            chunk, at = chunk_of(before + tap)
            rows = slice(at * half, (at + 1) * half)
            kept[chunk][rows, :] = jnp.where(core == 1, high, low)
            sent[chunk][rows, :] = jnp.where(core == 1, low, high)


def prepare(scal, labels_in, flow_in, winner_in, taps_in, lines, *refs):
    labels, flow, winner, taps, sems = refs[-5:]
    copies = [
        pltpu.make_async_copy(source, target, sems.at[index])
        for index, (source, target) in enumerate(
            ((labels_in, labels), (flow_in, flow), (winner_in, winner), (taps_in, taps))
        )
    ]
    for copy in copies:
        copy.start()
    for copy in copies[:3]:
        copy.wait()
    height, width = labels.shape
    blocks = winner.shape[1]
    at = lax.broadcasted_iota(jnp.int32, (blocks, width), 1)
    block = lax.broadcasted_iota(jnp.int32, (blocks, width), 0)
    spread = ((at >= block * BLK) & (at < block * BLK + BLK)).astype(BF16)
    fields = [labels[...].astype(F32)]
    ids = [
        jnp.dot(winner[row : row + 1, :].astype(F32).astype(BF16), spread, preferred_element_type=F32)
        for row in range(height // BLK)
    ]
    fields.append(jnp.concatenate([jnp.broadcast_to(part, (BLK, width)) for part in ids], axis=0))
    for index in range(2):
        rest = flow[index]
        for _ in range(3):
            piece = rest.astype(BF16).astype(F32)
            fields.append(piece)
            rest = rest - piece
    for row in range(height):
        lines[row] = jnp.concatenate([field[row : row + 1] for field in fields], axis=0).astype(BF16)
    copies[3].wait()
    layers = taps.shape[0]
    turned, sends = refs[:layers], refs[layers:-5]
    for layer in range(layers):
        for tap in range(9):
            block = taps[layer, tap].T
            half = block.shape[0] // 2
            turned[layer][tap] = block
            if sends:
                sends[layer][tap] = jnp.where(scal[1] == 0, block[:half], block[half:])


def first_layer(geom, scal, mid, top, bottom, tiles, *refs):
    taps = refs[:-7]
    padded, active, slope, mat, low, cen, high = refs[-7:]
    height, width, futs, layers = geom
    stride = width + SLOT
    halo = layers + 1
    col = scal[1]
    row_at = scal[2]
    row_count = scal[3]
    slots = height + 2 * halo
    tiles = [tiles[row * SLOT : (row + 1) * SLOT, :] for row in range(slots)]
    lane = lax.broadcasted_iota(jnp.int32, tiles[0].shape, 0)
    near = (lane < SLOT // 2).astype(jnp.int32) != col
    blank = jnp.zeros(tiles[0].shape, BF16)
    padded[:SLOT, :] = jnp.where(near & (col == 1), tiles[0], blank)
    for row in range(slots):
        at = SLOT + row * stride
        if row < halo:
            source = top[row * width : (row + 1) * width, :]
        elif row < halo + height:
            source = mid[row - halo]
        else:
            below = (row - halo - height) * width
            source = bottom[below : below + width, :]
        padded[at : at + width, :] = source
        after = tiles[row + 1] if row + 1 < slots else blank
        padded[at + width : at + stride, :] = jnp.where(
            near, jnp.where(col == 1, after, tiles[row]), blank
        )
    forward_taps(scal, taps, mat)
    spot = lax.broadcasted_iota(jnp.int32, (stride, active.shape[1]), 0)
    inside = (spot < width) | ((col == 0) & (spot < width + SLOT // 2)) | (
        (col == 1) & (spot >= width + SLOT // 2)
    )

    bump = ((spot >= width) & (col == 1)).astype(jnp.int32)

    def finish(at, size, keep):
        pre = combined(low, cen, high, at, size)
        sigma = jax.nn.sigmoid(pre)
        active[at : at + size, :] = jnp.where(keep, pre * sigma, 0.0).astype(BF16)
        return pre, sigma

    edge = halo - 1

    def finish_rows(begin, end):
        if begin == 0:
            finish(0, SLOT, (col == 1) & (row_at * height - edge >= 0))
        for row in range(begin, end):
            at = SLOT + row * stride
            place = row_at * height + row - edge
            keep = inside & (bump + place >= 0) & (bump + place < row_count * height)
            pre, sigma = finish(at, stride, keep)
            if edge <= row < edge + height:
                mine = (row - edge) * width
                own_pre = own_part(pre[:width], scal[0], futs)
                own_sig = own_part(sigma[:width], scal[0], futs)
                slope[mine : mine + width, :] = own_sig * (1.0 + own_pre * (1.0 - own_sig))

    convolve(padded, mat, low, cen, high, height + 2 * edge, 3, stride, finish_rows)


def cell_data(scal, lines, above, below, tile, height, width):
    stride = width + SLOT
    count = height + 2
    core, row_at, row_count = scal[1], scal[2], scal[3]
    beside = [block[block.shape[0] - 8 :, :width] for block in (above, below)]
    rows = beside[:1] + [lines[row] for row in range(height)] + beside[1:]
    blank = jnp.zeros((8, SLOT), F32)
    begin = tile.shape[0] - 8 * count
    tiles = [tile[begin + 8 * row : begin + 8 * row + 8, :SLOT].astype(F32) for row in range(count)]
    tiles = [blank, *tiles, blank]
    parts = []
    for row in range(count + 1):
        parts.append(jnp.where(core == 1, tiles[row + 1], tiles[row]))
        if row < count:
            parts.append(rows[row].astype(F32))
    flat = jnp.concatenate(parts, axis=1)
    place = lax.broadcasted_iota(jnp.int32, (8, flat.shape[1]), 1)
    line = jnp.full_like(place, -2)
    spot = place
    for row in range(count + 1):
        begin = row * stride
        line = jnp.where(place >= begin, row - 1, line)
        spot = jnp.where(place >= begin, place - (begin + SLOT), spot)
    main = spot >= 0
    right = (spot == -SLOT) & (core == 0)
    left = (spot == -1) & (core == 1)
    own = main & (line >= 0) & (line < height)
    line = line - right.astype(jnp.int32)
    at = row_at * height + line
    real = (at >= 0) & (at < row_count * height) & (line >= -1) & (line <= height)
    valid = real & (main | right | left)
    return (
        flat[0:1],
        flat[2:3] + flat[3:4] + flat[4:5],
        flat[5:6] + flat[6:7] + flat[7:8],
        flat[1:2],
        jnp.where(valid, 1.0, 0.0)[:1],
        jnp.where(own, 1.0, 0.0)[:1],
    )


def last_layer(
    geom, scale, scal, active, slope, padded, heads_w, lines, above, below, tile, *refs
):
    count = len(CHUNKS)
    taps, outs = refs[: -(10 + 2 * count)], refs[-(10 + 2 * count) : -9]
    kept, sent, small = outs[:count], outs[count:-1], outs[-1]
    mat, low, cen, high, out, bend, grad, own_grad, back_mat = refs[-9:]
    height, width, futs, layers = geom
    stride = width + SLOT
    count = grad.shape[0]
    forward_taps(scal, taps, mat)

    def finish_rows(begin, end):
        lo = SLOT + begin * stride if begin else 0
        for at, size in pieces(SLOT + end * stride - lo, stride):
            at += lo
            pre = combined(low, cen, high, at, size)
            sigma = jax.nn.sigmoid(pre)
            bend[at : at + size, :] = sigma * (1.0 + pre * (1.0 - sigma))
            out[at : at + size, :] = (pre * sigma).astype(BF16)

    convolve(active, mat, low, cen, high, height + 2, 4, stride, finish_rows)
    nfut = heads_w.shape[0] // 3
    heads = lax.dot_general(
        heads_w[...], out[...], (((1,), (1,)), ((), ())), preferred_element_type=F32
    )
    logit = heads[:nfut]
    target, flow_one, flow_two, picks, valid, own = cell_data(
        scal, lines, above, below, tile, height, width
    )
    first = heads[nfut : 2 * nfut] - flow_one
    second = heads[2 * nfut :] - flow_two
    future = lax.broadcasted_iota(jnp.int32, logit.shape, 0).astype(F32)
    mask = jnp.where(picks == future, valid, 0.0)
    cell = (
        jnp.maximum(logit, 0.0)
        + jnp.log1p(jnp.exp(-jnp.abs(logit)))
        - target * logit
        + 0.5 * (first * first + second * second)
    )
    loss = jnp.sum(jnp.where(mask * own > 0.0, cell, 0.0))
    picked = mask > 0.0
    grads = jnp.concatenate(
        [
            jnp.where(picked, (jax.nn.sigmoid(logit) - target) * scale, 0.0),
            jnp.where(picked, first * scale, 0.0),
            jnp.where(picked, second * scale, 0.0),
        ],
        axis=0,
    )
    mine = jnp.where(own > 0.0, grads, 0.0).astype(BF16)
    grads = grads.astype(BF16)
    by_head = jnp.dot(mine, out[...], preferred_element_type=F32)
    fut_here = nfut // futs
    lines = []
    for index in range(fut_here):
        for kind in range(3):
            at = kind * nfut + index
            line = by_head[at : at + 1, :]
            for part in range(1, futs):
                other = at + part * fut_here
                line = jnp.where(scal[0] == part, by_head[other : other + 1, :], line)
            lines.append(line)
    lines.append(jnp.broadcast_to(loss, (small.shape[0] - len(lines), small.shape[1])))
    totals = jnp.concatenate(lines, axis=0)
    small[...] = totals
    sent[0][kept[0].shape[0] :, :] = totals
    up = lax.dot_general(
        grads, heads_w[...], (((0,), (0,)), ((), ())), preferred_element_type=F32
    )
    low[: count, :] = up
    own_grad[...] = jnp.zeros_like(own_grad)

    def back(lo, size):
        value = (low[lo : lo + size, :] * bend[lo : lo + size, :]).astype(BF16)
        grad[lo : lo + size, :] = value
        return value

    back(0, SLOT)
    for row in range(height + 2):
        at = SLOT + row * stride
        value = back(at, stride)
        if 1 <= row <= height:
            mine_at = SLOT + (row - 1) * stride
            own_grad[mine_at : mine_at + width, :] = own_part(
                value[:width].astype(F32), scal[0], futs
            )
    kernel_grads(scal[1], own_grad, active, stride, stride, 0, kept, sent)
    back_layer(
        geom, scal, grad, taps, slope, padded, kept, sent, back_mat, low, cen, high,
        own_grad,
    )


def back_layer(
    geom, scal, grad, taps, slope, padded, kept, sent, mat, low, cen, high, own_grad
):
    height, width, futs, layers = geom
    stride = width + SLOT
    channels = grad.shape[1]
    own = channels // futs
    for tap in range(9):
        row, col = tap // 3, tap % 3
        mat[
            (2 - row) * channels : (3 - row) * channels, (2 - col) * own : (3 - col) * own
        ] = own_rows(forward_tap(tap, scal, taps), scal[0], futs).T
    own_grad[...] = jnp.zeros_like(own_grad)

    def finish_rows(begin, end):
        for row in range(begin, end):
            at = SLOT + row * stride
            up = (
                low[7 + at : 7 + at + width, :own]
                + cen[8 + at : 8 + at + width, :own]
                + high[9 + at : 9 + at + width, :own]
            )
            value = (up * slope[row * width : (row + 1) * width, :]).astype(BF16)
            own_grad[at : at + width, :] = value.astype(F32)

    convolve(grad, mat, low, cen, high, height, 4, stride, finish_rows)
    kernel_grads(scal[1], own_grad, padded, layers * stride, stride, 9, kept, sent)


def tap_parts(mine, got, after=None):
    if after is not None:
        got, _ = tied(got, after)
    return (mine, got, swap(got, "cols"))


def tied(*blocks):
    return lax.optimization_barrier(blocks)


def in_order(arrived, ready):
    return [
        tied(block, ready[index + 1])[0] if index + 1 < len(arrived) else block
        for index, block in enumerate(arrived)
    ]


def one_by_one(blocks, axis):
    arrived = []
    for block in blocks:
        if arrived:
            block = tied(block, arrived[-1])[0]
        arrived.append(swap(block, axis))
    return arrived


def split3(value):
    high = rounded(value)
    rest = value - high
    mid = rounded(rest)
    return [high.astype(BF16), mid.astype(BF16), rounded(rest - mid).astype(BF16)]


def joined(block, small):
    return jnp.concatenate([block.reshape(-1, block.shape[-1]), *split3(small)], axis=0)


def parted(block, like, small):
    size = block.shape[0] - 3 * small.shape[0]
    parts = block[size:].astype(F32).reshape(3, *small.shape)
    return block[:size].reshape(like.shape), small + (parts[0] + parts[1] + parts[2])


def tile_sums(kept, sent, small, core, row_at, half):
    bit = row_at & 1
    channels = small.shape[1]
    got = [swap(block, "cols") for block in sent]
    size = kept[0].shape[0]
    small = small + got[0][size:]
    got[0] = got[0][:size]
    blocks = [(mine + more).reshape(-1, half, channels) for mine, more in zip(kept, got)]
    half = half // 2
    kept = [jnp.where(bit == 1, block[:, half:], block[:, :half]) for block in blocks]
    sent = [jnp.where(bit == 1, block[:, :half], block[:, half:]) for block in blocks]
    ready = [rounded(block).astype(BF16) for block in sent]
    ready[0] = joined(ready[0], small)
    got = in_order([swap(block, "rows") for block in ready], ready)
    got[0], small = parted(got[0], kept[0], small)
    pairs = [rounded(mine + more.astype(F32)) for mine, more in zip(kept, got)]
    ready = [block.astype(BF16) for block in pairs]
    ready[0] = joined(ready[0], small)
    got = in_order([swap(block, "rows", 2) for block in ready], ready)
    got[0], small = parted(got[0], pairs[0], small)
    ready = [(mine + more.astype(F32)).astype(BF16) for mine, more in zip(pairs, got)]
    got = in_order([swap(block, "rows") for block in ready], ready)
    ready[-1], small = tied(ready[-1], small)
    ready = [ordered(bit == 1, mine, more, 1) for mine, more in zip(ready, got)]
    ready = [jnp.concatenate([ready[i] for i in group], axis=0) for group in ((0,), (1,), (2, 3))]
    got = in_order([swap(block, "cols") for block in ready], ready)
    return [ordered(core == 1, mine, more, 1) for mine, more in zip(ready, got)], small


def rounded(value):
    return lax.reduce_precision(value, 8, 7)


def local(features, trunk_weights, head_weights, flow_target, labels, winner):
    own, height, width = features.shape
    layers, _, _, channels = trunk_weights.shape
    fut_total = head_weights.shape[0]
    futs = lax.axis_size("futures")
    fut_here = fut_total // futs
    rows_total = lax.axis_size("rows")
    fut = lax.axis_index("futures")
    core = lax.axis_index("cols")
    row_at = lax.axis_index("rows")
    cell_count = height * width * rows_total * lax.axis_size("cols")
    scale = 1.0 / math.sqrt(cell_count)
    halo = layers + 1
    stride = width + SLOT
    geom = (height, width, futs, layers)
    scal = jnp.stack([fut, core, row_at, jnp.int32(rows_total)]).astype(jnp.int32)

    shape = jax.ShapeDtypeStruct
    mine = jnp.transpose(features, (1, 2, 0))
    half_taps = shape((9, channels // 2, own), BF16)
    lines, *turned = pl.pallas_call(
        prepare,
        out_shape=(shape((height, 8, width), BF16),)
        + (shape((9, channels, own), BF16),) * layers
        + ((half_taps,) * layers if futs == 2 else ()),
        in_specs=[SMEM] + [pl.BlockSpec(memory_space=pltpu.HBM)] * 4,
        out_specs=(VMEM,) * (1 + layers + (layers if futs == 2 else 0)),
        scratch_shapes=[
            pltpu.VMEM(labels.shape, labels.dtype),
            pltpu.VMEM(flow_target.shape, F32),
            pltpu.VMEM(winner.shape, winner.dtype),
            pltpu.VMEM(trunk_weights.shape, BF16),
            pltpu.SemaphoreType.DMA((4,)),
        ],
        compiler_params=limited(4),
        name="prepare",
    )(
        scal,
        *[
            pltpu.with_memory_space_constraint(array, pltpu.HBM)
            for array in (labels, flow_target, winner, trunk_weights)
        ],
    )
    if futs == 2:
        outer = jnp.concatenate([mine[:halo], mine[-halo:]], axis=0)
        theirs = swap(outer, "futures")
        outer = ordered(fut == 1, outer, theirs, 2)
        sends = tied(theirs, *turned[layers + 1 :])[1:]
        inner = tied(mine[halo:-halo], lines)[0]
        inner_theirs = swap(inner, "futures")
        first, last = outer[:halo], outer[halo:]
        got_taps = [swap(send, "futures") for send in [turned[layers], *sends]]
        taps = tap_parts(turned[0], got_taps[0])
    else:
        mid = lax.all_gather(mine, "futures", axis=2, tiled=True)
        first, last = mid[:halo], mid[-halo:]
        whole_taps = lax.all_gather(trunk_weights, "futures", axis=2, tiled=True)
        taps = (whole_taps[0],)

    def with_line(block, line):
        line = jnp.pad(line, ((0, 0), (0, channels - width)))
        return jnp.concatenate([block.reshape(-1, channels), line], axis=0)

    top, bottom = tied(with_line(last, lines[-1]), with_line(first, lines[0]))
    top, bottom = shift(top, "rows", 1), shift(bottom, "rows", -1)
    if futs == 2:
        top, bottom, inner_theirs = tied(top, bottom, inner_theirs)
        inner = ordered(fut == 1, inner, inner_theirs, 2)
        mid = jnp.concatenate([first, inner, last], axis=0)

    def halo_rows(block):
        return block[: halo * width].reshape(halo, width, channels)

    def line_of(block):
        return block[halo * width :, :width]

    def edge_of(block):
        return jnp.where(core == 0, block[..., -SLOT:, :], block[..., :SLOT, :])

    line_rows = jnp.concatenate([line_of(top)[None], lines, line_of(bottom)[None]], axis=0)
    edges = jnp.where(core == 0, line_rows[:, :, -SLOT:], line_rows[:, :, :SLOT])
    edges = jnp.pad(edges.reshape(-1, SLOT), ((0, 0), (0, channels - SLOT)))
    blocks = [edge_of(halo_rows(top)), edge_of(mid), edge_of(halo_rows(bottom))]
    tiles = swap(
        jnp.concatenate([block.reshape(-1, channels) for block in blocks] + [edges], axis=0),
        "cols",
    )
    heads_w = jnp.transpose(head_weights, (1, 0, 2)).reshape(3 * fut_total, channels)

    def cells(rows):
        return SLOT + rows * stride

    first_cells = cells(height + 4)
    last_cells = cells(height + 2)
    own_cells = -(-cells(height) // 128) * 128
    padded, active, slope = pl.pallas_call(
        functools.partial(first_layer, geom),
        out_shape=(
            shape((cells(height + 6), channels), BF16),
            shape((first_cells, channels), BF16),
            shape((height * width, own), F32),
        ),
        in_specs=[SMEM] + [VMEM] * (4 + len(taps)),
        out_specs=(VMEM,) * 3,
        scratch_shapes=[pltpu.VMEM((3 * channels, 3 * channels), BF16)]
        + [pltpu.VMEM((first_cells + 16, channels), F32)] * 3,
        compiler_params=limited(8),
        name="first_layer",
    )(scal, mid, top, bottom, tiles, *taps)

    if futs == 2:
        taps = tap_parts(turned[layers - 1], got_taps[layers - 1], active)
    else:
        taps = (whole_taps[layers - 1],)
    lines_out = -(-(3 * fut_here + 1) // 8) * 8
    sizes = [size * (own // 2) for size in CHUNKS]
    kept_out = tuple(shape((size, channels), F32) for size in sizes)
    sizes[0] += lines_out
    sent_out = tuple(shape((size, channels), F32) for size in sizes)
    *parts, small = pl.pallas_call(
        functools.partial(last_layer, geom, scale),
        out_shape=kept_out + sent_out + (shape((lines_out, channels), F32),),
        in_specs=[SMEM] + [VMEM] * (8 + len(taps)),
        out_specs=(VMEM,) * (2 * len(CHUNKS) + 1),
        scratch_shapes=[pltpu.VMEM((3 * channels, 3 * channels), BF16)]
        + [pltpu.VMEM((last_cells + 16, channels), F32)] * 3
        + [
            pltpu.VMEM((last_cells, channels), BF16),
            pltpu.VMEM((last_cells, channels), F32),
            pltpu.VMEM((last_cells, channels), BF16),
            pltpu.VMEM((own_cells, own), F32),
            pltpu.VMEM((3 * channels, 3 * own), BF16),
        ],
        compiler_params=limited(12),
        name="last_layer",
    )(scal, active, slope, padded, heads_w, lines, top, bottom, tiles, *taps)

    kept, sent = parts[: len(CHUNKS)], parts[len(CHUNKS) :]
    if rows_total == 4:
        sums, small = tile_sums(kept, sent, small, core, row_at, own // 2)
    else:
        sent[0] = sent[0][:-lines_out]
        sums = [
            ordered(core == 1, *[part.reshape(-1, own // 2, channels) for part in both], 1)
            for both in zip(kept, sent)
        ]
        sums, small = lax.psum((sums, small), ("rows", "cols"))
    taps_of = []
    for layer in range(layers):
        low = 9 * (layers - 1 - layer)
        begin = 0
        for block in sums:
            first = max(low - begin, 0)
            last = min(low + 9 - begin, block.shape[0])
            if first < last:
                taps_of.append(block[first:last])
            begin += block.shape[0]
    trunk_grad = jnp.concatenate(taps_of, axis=0).astype(F32).reshape(layers, 9, own, channels)
    head_grad = small[: 3 * fut_here].reshape(fut_here, 3, channels)
    total = small[3 * fut_here, :1] / cell_count
    return (total, trunk_grad, head_grad)


def solution(mesh):
    placed = (
        P("futures", ("groups", "rows"), "cols"),
        P(None, None, "futures", None),
        P(),
        P(None, ("groups", "rows"), "cols"),
        P(("groups", "rows"), "cols"),
        P(("groups", "rows"), "cols"),
    )
    return jax.shard_map(
        local,
        mesh=mesh,
        in_specs=placed,
        out_specs=(P("groups"), P("groups", None, "futures", None), P("futures", "groups", None)),
        check_vma=False,
    )
```

```python
import functools
import math

import jax
import jax.numpy as jnp
from jax import lax
from jax.experimental import pallas as pl
from jax.experimental.pallas import tpu as pltpu
from jax.sharding import PartitionSpec as P

BLK = 8
SLOT = 16
CHUNKS = (5, 4, 4, 5)
F32 = jnp.float32
BF16 = jnp.bfloat16
VMEM = pl.BlockSpec(memory_space=pltpu.VMEM)
SMEM = pl.BlockSpec(memory_space=pltpu.SMEM)


def limited(mebibytes):
    return pltpu.CompilerParams(vmem_limit_bytes=mebibytes * 1024 * 1024)


def swap(block, axis, distance=1):
    count = lax.axis_size(axis)
    return lax.ppermute(block, axis, [(i, i ^ distance) for i in range(count)])


def shift(block, axis, step):
    count = lax.axis_size(axis)
    pairs = [(i, i + step) for i in range(count) if 0 <= i + step < count]
    return lax.ppermute(block, axis, pairs)


def ordered(flag, first, second, axis):
    return jnp.concatenate(
        [jnp.where(flag, second, first), jnp.where(flag, first, second)], axis=axis
    )


def pieces(total, step):
    return [(lo, min(step, total - lo)) for lo in range(0, total, step)]


def forward_tap(tap, scal, refs):
    if len(refs) == 1:
        return refs[0][tap].T
    own_ref, got_ref, mate_ref = refs
    theirs = ordered(scal[1] == 1, got_ref[tap], mate_ref[tap], 0)
    return ordered(scal[0] == 1, own_ref[tap], theirs, 1)


def forward_taps(scal, refs, mat_ref):
    for tap in range(9):
        row, col = tap // 3, tap % 3
        block = forward_tap(tap, scal, refs)
        channels = block.shape[0]
        mat_ref[
            row * channels : (row + 1) * channels, col * channels : (col + 1) * channels
        ] = block


def own_rows(value, index, count):
    size = value.shape[0] // count
    result = value[:size]
    for part in range(1, count):
        result = jnp.where(index == part, value[part * size : (part + 1) * size], result)
    return result


def clear_ends(low_ref, high_ref, count):
    blank = jnp.zeros((8, low_ref.shape[1]), F32)
    low_ref[:8, :] = blank
    high_ref[8 + count : 16 + count, :] = blank


def row_groups(count, size):
    return [(lo, min(lo + size, count)) for lo in range(0, count, size)]


def convolve(src_ref, mat_ref, low_ref, mid_ref, high_ref, rows, group, stride, finish):
    channels = src_ref.shape[1]
    clear_ends(low_ref, high_ref, SLOT + rows * stride)
    waiting = None
    for first, last in row_groups(rows, group):
        lo = SLOT + first * stride if first else 0
        hi = SLOT + last * stride
        window = jnp.concatenate(
            [src_ref[lo + row * stride : hi + row * stride, :] for row in range(3)], axis=1
        )
        width = mat_ref.shape[1] // 3
        part = jnp.dot(window, mat_ref[...], preferred_element_type=F32)
        for col, ref in enumerate((low_ref, mid_ref, high_ref)):
            ref[8 + lo : 8 + hi, :width] = part[:, col * width : (col + 1) * width]
        if waiting is not None:
            finish(*waiting)
        waiting = (first, last)
    finish(*waiting)


def combined(low_ref, mid_ref, high_ref, lo, size):
    return (
        low_ref[7 + lo : 7 + lo + size, :]
        + mid_ref[8 + lo : 8 + lo + size, :]
        + high_ref[9 + lo : 9 + lo + size, :]
    )


def own_part(value, index, count):
    width = value.shape[1] // count
    result = value[:, :width]
    for part in range(1, count):
        result = jnp.where(index == part, value[:, part * width : (part + 1) * width], result)
    return result


def chunk_of(index):
    for chunk, size in enumerate(CHUNKS):
        if index < size:
            return chunk, index
        index -= size


def kernel_grads(core, grad_ref, src_ref, base, stride, before, kept, sent):
    own = grad_ref.shape[1]
    cells = grad_ref.shape[0]
    turned = grad_ref[...].T.astype(BF16)
    moved = jnp.concatenate(
        [
            pltpu.roll(turned, cells - 1, 1),
            turned,
            pltpu.roll(turned, 1, 1),
        ],
        axis=0,
    )
    for row in range(3):
        start = base + row * stride
        part = jnp.dot(moved, src_ref[start : start + cells, :], preferred_element_type=F32)
        for col in range(3):
            tap = 3 * row + col
            half = own // 2
            low = part[col * own : col * own + half, :]
            high = part[col * own + half : (col + 1) * own, :]
            chunk, at = chunk_of(before + tap)
            rows = slice(at * half, (at + 1) * half)
            kept[chunk][rows, :] = jnp.where(core == 1, high, low)
            sent[chunk][rows, :] = jnp.where(core == 1, low, high)


def prepare(scal, labels_in, flow_in, winner_in, taps_in, lines, *refs):
    labels, flow, winner, taps, sems = refs[-5:]
    copies = [
        pltpu.make_async_copy(source, target, sems.at[index])
        for index, (source, target) in enumerate(
            ((labels_in, labels), (flow_in, flow), (winner_in, winner), (taps_in, taps))
        )
    ]
    for copy in copies:
        copy.start()
    for copy in copies[:3]:
        copy.wait()
    height, width = labels.shape
    blocks = winner.shape[1]
    at = lax.broadcasted_iota(jnp.int32, (blocks, width), 1)
    block = lax.broadcasted_iota(jnp.int32, (blocks, width), 0)
    spread = ((at >= block * BLK) & (at < block * BLK + BLK)).astype(BF16)
    fields = [labels[...].astype(F32)]
    ids = [
        jnp.dot(winner[row : row + 1, :].astype(F32).astype(BF16), spread, preferred_element_type=F32)
        for row in range(height // BLK)
    ]
    fields.append(jnp.concatenate([jnp.broadcast_to(part, (BLK, width)) for part in ids], axis=0))
    for index in range(2):
        rest = flow[index]
        for _ in range(3):
            piece = rest.astype(BF16).astype(F32)
            fields.append(piece)
            rest = rest - piece
    for row in range(height):
        lines[row] = jnp.concatenate([field[row : row + 1] for field in fields], axis=0).astype(BF16)
    copies[3].wait()
    layers = taps.shape[0]
    turned, sends = refs[:layers], refs[layers:-5]
    for layer in range(layers):
        for tap in range(9):
            block = taps[layer, tap].T
            half = block.shape[0] // 2
            turned[layer][tap] = block
            if sends:
                sends[layer][tap] = jnp.where(scal[1] == 0, block[:half], block[half:])


def first_layer(geom, scal, mid, top, bottom, tiles, *refs):
    taps = refs[:-7]
    padded, active, slope, mat, low, cen, high = refs[-7:]
    height, width, futs, layers = geom
    stride = width + SLOT
    halo = layers + 1
    col = scal[1]
    row_at = scal[2]
    row_count = scal[3]
    slots = height + 2 * halo
    tiles = [tiles[row * SLOT : (row + 1) * SLOT, :] for row in range(slots)]
    lane = lax.broadcasted_iota(jnp.int32, tiles[0].shape, 0)
    near = (lane < SLOT // 2).astype(jnp.int32) != col
    blank = jnp.zeros(tiles[0].shape, BF16)
    padded[:SLOT, :] = jnp.where(near & (col == 1), tiles[0], blank)
    for row in range(slots):
        at = SLOT + row * stride
        if row < halo:
            source = top[row * width : (row + 1) * width, :]
        elif row < halo + height:
            source = mid[row - halo]
        else:
            below = (row - halo - height) * width
            source = bottom[below : below + width, :]
        padded[at : at + width, :] = source
        after = tiles[row + 1] if row + 1 < slots else blank
        padded[at + width : at + stride, :] = jnp.where(
            near, jnp.where(col == 1, after, tiles[row]), blank
        )
    forward_taps(scal, taps, mat)
    spot = lax.broadcasted_iota(jnp.int32, (stride, active.shape[1]), 0)
    inside = (spot < width) | ((col == 0) & (spot < width + SLOT // 2)) | (
        (col == 1) & (spot >= width + SLOT // 2)
    )

    bump = ((spot >= width) & (col == 1)).astype(jnp.int32)

    def finish(at, size, keep):
        pre = combined(low, cen, high, at, size)
        sigma = jax.nn.sigmoid(pre)
        active[at : at + size, :] = jnp.where(keep, pre * sigma, 0.0).astype(BF16)
        return pre, sigma

    edge = halo - 1

    def finish_rows(begin, end):
        if begin == 0:
            finish(0, SLOT, (col == 1) & (row_at * height - edge >= 0))
        for row in range(begin, end):
            at = SLOT + row * stride
            place = row_at * height + row - edge
            keep = inside & (bump + place >= 0) & (bump + place < row_count * height)
            pre, sigma = finish(at, stride, keep)
            if edge <= row < edge + height:
                mine = (row - edge) * width
                own_pre = own_part(pre[:width], scal[0], futs)
                own_sig = own_part(sigma[:width], scal[0], futs)
                slope[mine : mine + width, :] = own_sig * (1.0 + own_pre * (1.0 - own_sig))

    convolve(padded, mat, low, cen, high, height + 2 * edge, 3, stride, finish_rows)


def cell_data(scal, lines, above, below, tile, height, width):
    stride = width + SLOT
    count = height + 2
    core, row_at, row_count = scal[1], scal[2], scal[3]
    beside = [block[block.shape[0] - 8 :, :width] for block in (above, below)]
    rows = beside[:1] + [lines[row] for row in range(height)] + beside[1:]
    blank = jnp.zeros((8, SLOT), F32)
    begin = tile.shape[0] - 8 * count
    tiles = [tile[begin + 8 * row : begin + 8 * row + 8, :SLOT].astype(F32) for row in range(count)]
    tiles = [blank, *tiles, blank]
    parts = []
    for row in range(count + 1):
        parts.append(jnp.where(core == 1, tiles[row + 1], tiles[row]))
        if row < count:
            parts.append(rows[row].astype(F32))
    flat = jnp.concatenate(parts, axis=1)
    place = lax.broadcasted_iota(jnp.int32, (8, flat.shape[1]), 1)
    line = jnp.full_like(place, -2)
    spot = place
    for row in range(count + 1):
        begin = row * stride
        line = jnp.where(place >= begin, row - 1, line)
        spot = jnp.where(place >= begin, place - (begin + SLOT), spot)
    main = spot >= 0
    right = (spot == -SLOT) & (core == 0)
    left = (spot == -1) & (core == 1)
    own = main & (line >= 0) & (line < height)
    line = line - right.astype(jnp.int32)
    at = row_at * height + line
    real = (at >= 0) & (at < row_count * height) & (line >= -1) & (line <= height)
    valid = real & (main | right | left)
    return (
        flat[0:1],
        flat[2:3] + flat[3:4] + flat[4:5],
        flat[5:6] + flat[6:7] + flat[7:8],
        flat[1:2],
        jnp.where(valid, 1.0, 0.0)[:1],
        jnp.where(own, 1.0, 0.0)[:1],
    )


def last_layer(
    geom, scale, scal, active, slope, padded, heads_w, lines, above, below, tile, *refs
):
    count = len(CHUNKS)
    taps, outs = refs[: -(10 + 2 * count)], refs[-(10 + 2 * count) : -9]
    kept, sent, small = outs[:count], outs[count:-1], outs[-1]
    mat, low, cen, high, out, bend, grad, own_grad, back_mat = refs[-9:]
    height, width, futs, layers = geom
    stride = width + SLOT
    count = grad.shape[0]
    forward_taps(scal, taps, mat)

    def finish_rows(begin, end):
        lo = SLOT + begin * stride if begin else 0
        for at, size in pieces(SLOT + end * stride - lo, stride):
            at += lo
            pre = combined(low, cen, high, at, size)
            sigma = jax.nn.sigmoid(pre)
            bend[at : at + size, :] = sigma * (1.0 + pre * (1.0 - sigma))
            out[at : at + size, :] = (pre * sigma).astype(BF16)

    convolve(active, mat, low, cen, high, height + 2, 4, stride, finish_rows)
    nfut = heads_w.shape[0] // 3
    heads = lax.dot_general(
        heads_w[...], out[...], (((1,), (1,)), ((), ())), preferred_element_type=F32
    )
    logit = heads[:nfut]
    target, flow_one, flow_two, picks, valid, own = cell_data(
        scal, lines, above, below, tile, height, width
    )
    first = heads[nfut : 2 * nfut] - flow_one
    second = heads[2 * nfut :] - flow_two
    future = lax.broadcasted_iota(jnp.int32, logit.shape, 0).astype(F32)
    mask = jnp.where(picks == future, valid, 0.0)
    cell = (
        jnp.maximum(logit, 0.0)
        + jnp.log1p(jnp.exp(-jnp.abs(logit)))
        - target * logit
        + 0.5 * (first * first + second * second)
    )
    loss = jnp.sum(jnp.where(mask * own > 0.0, cell, 0.0))
    picked = mask > 0.0
    grads = jnp.concatenate(
        [
            jnp.where(picked, (jax.nn.sigmoid(logit) - target) * scale, 0.0),
            jnp.where(picked, first * scale, 0.0),
            jnp.where(picked, second * scale, 0.0),
        ],
        axis=0,
    )
    mine = jnp.where(own > 0.0, grads, 0.0).astype(BF16)
    grads = grads.astype(BF16)
    by_head = jnp.dot(mine, out[...], preferred_element_type=F32)
    fut_here = nfut // futs
    lines = []
    for index in range(fut_here):
        for kind in range(3):
            at = kind * nfut + index
            line = by_head[at : at + 1, :]
            for part in range(1, futs):
                other = at + part * fut_here
                line = jnp.where(scal[0] == part, by_head[other : other + 1, :], line)
            lines.append(line)
    lines.append(jnp.broadcast_to(loss, (small.shape[0] - len(lines), small.shape[1])))
    totals = jnp.concatenate(lines, axis=0)
    small[...] = totals
    sent[0][kept[0].shape[0] :, :] = totals
    up = lax.dot_general(
        grads, heads_w[...], (((0,), (0,)), ((), ())), preferred_element_type=F32
    )
    low[: count, :] = up
    own_grad[...] = jnp.zeros_like(own_grad)

    def back(lo, size):
        value = (low[lo : lo + size, :] * bend[lo : lo + size, :]).astype(BF16)
        grad[lo : lo + size, :] = value
        return value

    back(0, SLOT)
    for row in range(height + 2):
        at = SLOT + row * stride
        value = back(at, stride)
        if 1 <= row <= height:
            mine_at = SLOT + (row - 1) * stride
            own_grad[mine_at : mine_at + width, :] = own_part(
                value[:width].astype(F32), scal[0], futs
            )
    kernel_grads(scal[1], own_grad, active, stride, stride, 0, kept, sent)
    back_layer(
        geom, scal, grad, taps, slope, padded, kept, sent, back_mat, low, cen, high,
        own_grad,
    )


def back_layer(
    geom, scal, grad, taps, slope, padded, kept, sent, mat, low, cen, high, own_grad
):
    height, width, futs, layers = geom
    stride = width + SLOT
    channels = grad.shape[1]
    own = channels // futs
    for tap in range(9):
        row, col = tap // 3, tap % 3
        mat[
            (2 - row) * channels : (3 - row) * channels, (2 - col) * own : (3 - col) * own
        ] = own_rows(forward_tap(tap, scal, taps), scal[0], futs).T
    own_grad[...] = jnp.zeros_like(own_grad)

    def finish_rows(begin, end):
        for row in range(begin, end):
            at = SLOT + row * stride
            up = (
                low[7 + at : 7 + at + width, :own]
                + cen[8 + at : 8 + at + width, :own]
                + high[9 + at : 9 + at + width, :own]
            )
            value = (up * slope[row * width : (row + 1) * width, :]).astype(BF16)
            own_grad[at : at + width, :] = value.astype(F32)

    convolve(grad, mat, low, cen, high, height, 4, stride, finish_rows)
    kernel_grads(scal[1], own_grad, padded, layers * stride, stride, 9, kept, sent)


def tap_parts(mine, got, after=None):
    if after is not None:
        got, _ = tied(got, after)
    return (mine, got, swap(got, "cols"))


def tied(*blocks):
    return lax.optimization_barrier(blocks)


def in_order(arrived, ready):
    return [
        tied(block, ready[index + 1])[0] if index + 1 < len(arrived) else block
        for index, block in enumerate(arrived)
    ]


def one_by_one(blocks, axis):
    arrived = []
    for block in blocks:
        if arrived:
            block = tied(block, arrived[-1])[0]
        arrived.append(swap(block, axis))
    return arrived


def split3(value):
    high = rounded(value)
    rest = value - high
    mid = rounded(rest)
    return [high.astype(BF16), mid.astype(BF16), rounded(rest - mid).astype(BF16)]


def joined(block, small):
    return jnp.concatenate([block.reshape(-1, block.shape[-1]), *split3(small)], axis=0)


def parted(block, like, small):
    size = block.shape[0] - 3 * small.shape[0]
    parts = block[size:].astype(F32).reshape(3, *small.shape)
    return block[:size].reshape(like.shape), small + (parts[0] + parts[1] + parts[2])


def tile_sums(kept, sent, small, core, row_at, half):
    bit = row_at & 1
    channels = small.shape[1]
    got = [swap(block, "cols") for block in sent]
    size = kept[0].shape[0]
    small = small + got[0][size:]
    got[0] = got[0][:size]
    blocks = [(mine + more).reshape(-1, half, channels) for mine, more in zip(kept, got)]
    half = half // 2
    kept = [jnp.where(bit == 1, block[:, half:], block[:, :half]) for block in blocks]
    sent = [jnp.where(bit == 1, block[:, :half], block[:, half:]) for block in blocks]
    ready = [rounded(block).astype(BF16) for block in sent]
    ready[0] = joined(ready[0], small)
    got = in_order([swap(block, "rows") for block in ready], ready)
    got[0], small = parted(got[0], kept[0], small)
    pairs = [rounded(mine + more.astype(F32)) for mine, more in zip(kept, got)]
    ready = [block.astype(BF16) for block in pairs]
    ready[0] = joined(ready[0], small)
    got = in_order([swap(block, "rows", 2) for block in ready], ready)
    got[0], small = parted(got[0], pairs[0], small)
    ready = [(mine + more.astype(F32)).astype(BF16) for mine, more in zip(pairs, got)]
    got = in_order([swap(block, "rows") for block in ready], ready)
    ready[-1], small = tied(ready[-1], small)
    ready = [ordered(bit == 1, mine, more, 1) for mine, more in zip(ready, got)]
    ready = [jnp.concatenate([ready[i] for i in group], axis=0) for group in ((0,), (1,), (2, 3))]
    got = in_order([swap(block, "cols") for block in ready], ready)
    return [ordered(core == 1, mine, more, 1) for mine, more in zip(ready, got)], small


def rounded(value):
    return lax.reduce_precision(value, 8, 7)


def local(features, trunk_weights, head_weights, flow_target, labels, winner):
    own, height, width = features.shape
    layers, _, _, channels = trunk_weights.shape
    fut_total = head_weights.shape[0]
    futs = lax.axis_size("futures")
    fut_here = fut_total // futs
    rows_total = lax.axis_size("rows")
    fut = lax.axis_index("futures")
    core = lax.axis_index("cols")
    row_at = lax.axis_index("rows")
    cell_count = height * width * rows_total * lax.axis_size("cols")
    scale = 1.0 / math.sqrt(cell_count)
    halo = layers + 1
    stride = width + SLOT
    geom = (height, width, futs, layers)
    scal = jnp.stack([fut, core, row_at, jnp.int32(rows_total)]).astype(jnp.int32)

    shape = jax.ShapeDtypeStruct
    mine = jnp.transpose(features, (1, 2, 0))
    half_taps = shape((9, channels // 2, own), BF16)
    lines, *turned = pl.pallas_call(
        prepare,
        out_shape=(shape((height, 8, width), BF16),)
        + (shape((9, channels, own), BF16),) * layers
        + ((half_taps,) * layers if futs == 2 else ()),
        in_specs=[SMEM] + [pl.BlockSpec(memory_space=pltpu.HBM)] * 4,
        out_specs=(VMEM,) * (1 + layers + (layers if futs == 2 else 0)),
        scratch_shapes=[
            pltpu.VMEM(labels.shape, labels.dtype),
            pltpu.VMEM(flow_target.shape, F32),
            pltpu.VMEM(winner.shape, winner.dtype),
            pltpu.VMEM(trunk_weights.shape, BF16),
            pltpu.SemaphoreType.DMA((4,)),
        ],
        compiler_params=limited(4),
        name="prepare",
    )(
        scal,
        *[
            pltpu.with_memory_space_constraint(array, pltpu.HBM)
            for array in (labels, flow_target, winner, trunk_weights)
        ],
    )
    if futs == 2:
        outer = jnp.concatenate([mine[:halo], mine[-halo:]], axis=0)
        theirs = swap(outer, "futures")
        outer = ordered(fut == 1, outer, theirs, 2)
        sends = tied(theirs, *turned[layers + 1 :])[1:]
        inner = tied(mine[halo:-halo], lines)[0]
        inner_theirs = swap(inner, "futures")
        first, last = outer[:halo], outer[halo:]
        got_taps = [swap(send, "futures") for send in [turned[layers], *sends]]
        taps = tap_parts(turned[0], got_taps[0])
    else:
        mid = lax.all_gather(mine, "futures", axis=2, tiled=True)
        first, last = mid[:halo], mid[-halo:]
        whole_taps = lax.all_gather(trunk_weights, "futures", axis=2, tiled=True)
        taps = (whole_taps[0],)

    def with_line(block, line):
        line = jnp.pad(line, ((0, 0), (0, channels - width)))
        return jnp.concatenate([block.reshape(-1, channels), line], axis=0)

    top, bottom = tied(with_line(last, lines[-1]), with_line(first, lines[0]))
    top, bottom = shift(top, "rows", 1), shift(bottom, "rows", -1)
    if futs == 2:
        top, bottom, inner_theirs = tied(top, bottom, inner_theirs)
        inner = ordered(fut == 1, inner, inner_theirs, 2)
        mid = jnp.concatenate([first, inner, last], axis=0)

    def halo_rows(block):
        return block[: halo * width].reshape(halo, width, channels)

    def line_of(block):
        return block[halo * width :, :width]

    def edge_of(block):
        return jnp.where(core == 0, block[..., -SLOT:, :], block[..., :SLOT, :])

    line_rows = jnp.concatenate([line_of(top)[None], lines, line_of(bottom)[None]], axis=0)
    edges = jnp.where(core == 0, line_rows[:, :, -SLOT:], line_rows[:, :, :SLOT])
    edges = jnp.pad(edges.reshape(-1, SLOT), ((0, 0), (0, channels - SLOT)))
    blocks = [edge_of(halo_rows(top)), edge_of(mid), edge_of(halo_rows(bottom))]
    tiles = swap(
        jnp.concatenate([block.reshape(-1, channels) for block in blocks] + [edges], axis=0),
        "cols",
    )
    heads_w = jnp.transpose(head_weights, (1, 0, 2)).reshape(3 * fut_total, channels)

    def cells(rows):
        return SLOT + rows * stride

    first_cells = cells(height + 4)
    last_cells = cells(height + 2)
    own_cells = -(-cells(height) // 128) * 128
    padded, active, slope = pl.pallas_call(
        functools.partial(first_layer, geom),
        out_shape=(
            shape((cells(height + 6), channels), BF16),
            shape((first_cells, channels), BF16),
            shape((height * width, own), F32),
        ),
        in_specs=[SMEM] + [VMEM] * (4 + len(taps)),
        out_specs=(VMEM,) * 3,
        scratch_shapes=[pltpu.VMEM((3 * channels, 3 * channels), BF16)]
        + [pltpu.VMEM((first_cells + 16, channels), F32)] * 3,
        compiler_params=limited(8),
        name="first_layer",
    )(scal, mid, top, bottom, tiles, *taps)

    if futs == 2:
        taps = tap_parts(turned[layers - 1], got_taps[layers - 1], active)
    else:
        taps = (whole_taps[layers - 1],)
    lines_out = -(-(3 * fut_here + 1) // 8) * 8
    sizes = [size * (own // 2) for size in CHUNKS]
    kept_out = tuple(shape((size, channels), F32) for size in sizes)
    sizes[0] += lines_out
    sent_out = tuple(shape((size, channels), F32) for size in sizes)
    *parts, small = pl.pallas_call(
        functools.partial(last_layer, geom, scale),
        out_shape=kept_out + sent_out + (shape((lines_out, channels), F32),),
        in_specs=[SMEM] + [VMEM] * (8 + len(taps)),
        out_specs=(VMEM,) * (2 * len(CHUNKS) + 1),
        scratch_shapes=[pltpu.VMEM((3 * channels, 3 * channels), BF16)]
        + [pltpu.VMEM((last_cells + 16, channels), F32)] * 3
        + [
            pltpu.VMEM((last_cells, channels), BF16),
            pltpu.VMEM((last_cells, channels), F32),
            pltpu.VMEM((last_cells, channels), BF16),
            pltpu.VMEM((own_cells, own), F32),
            pltpu.VMEM((3 * channels, 3 * own), BF16),
        ],
        compiler_params=limited(12),
        name="last_layer",
    )(scal, active, slope, padded, heads_w, lines, top, bottom, tiles, *taps)

    kept, sent = parts[: len(CHUNKS)], parts[len(CHUNKS) :]
    if rows_total == 4:
        sums, small = tile_sums(kept, sent, small, core, row_at, own // 2)
    else:
        sent[0] = sent[0][:-lines_out]
        sums = [
            ordered(core == 1, *[part.reshape(-1, own // 2, channels) for part in both], 1)
            for both in zip(kept, sent)
        ]
        sums, small = lax.psum((sums, small), ("rows", "cols"))
    taps_of = []
    for layer in range(layers):
        low = 9 * (layers - 1 - layer)
        begin = 0
        for block in sums:
            first = max(low - begin, 0)
            last = min(low + 9 - begin, block.shape[0])
            if first < last:
                taps_of.append(block[first:last])
            begin += block.shape[0]
    trunk_grad = jnp.concatenate(taps_of, axis=0).astype(F32).reshape(layers, 9, own, channels)
    head_grad = small[: 3 * fut_here].reshape(fut_here, 3, channels)
    total = small[3 * fut_here, :1] / cell_count
    return (total, trunk_grad, head_grad)


def solution(mesh):
    placed = (
        P("futures", ("groups", "rows"), "cols"),
        P(None, None, "futures", None),
        P(),
        P(None, ("groups", "rows"), "cols"),
        P(("groups", "rows"), "cols"),
        P(("groups", "rows"), "cols"),
    )
    return jax.shard_map(
        local,
        mesh=mesh,
        in_specs=placed,
        out_specs=(P("groups"), P("groups", None, "futures", None), P("futures", "groups", None)),
        check_vma=False,
    )
```
